256 devices in a mesh: docs: 64 (over y, z, core), mp: 4 (over x).
Axes of the slice: x: 4, y: 4, z: 8, core: 2. Of those that a mesh axis runs over, the one named last changes fastest.
Arguments:
- queries: bfloat16 [16384, 8192], P('docs', 'mp'), may hold values from -8 to 8
- keys: bfloat16 [204928, 1024], P('docs', 'mp'), may hold values from -6 to 6
- values: bfloat16 [204928, 1024], P('docs', 'mp'), may hold values from -9 to 9
- owner_of_row: int32 [16384, 1], P('docs'), may hold values from 0 to 63; in each aligned block of 256 rows (0 to 255, 256 to 511, ...) at most 6 rows name the same one
- visible: int32 [16384], P('docs'), may hold values from 1 to 2
- gain: bfloat16 [8192], P('mp'), may hold values from 0.099609375 to 1.8984375
Outputs:
- attended: bfloat16 [16384, 8192], P('docs', 'mp')
The draws below stay inside these ranges and needn't reach their ends.
Inputs may be any that keep to these rules, and one draw needn't show every extreme that they name: `owner_of_row`: among the rows of one index of docs (aligned blocks of 256 rows), no owner is named by more than 6 rows, a bound that some block reaches.
All inputs are finite; a program needn't handle non-finite values.
Results may differ from the reference program's by a relative error of at most 0.0056.
Values may be sent and summed in bfloat16 or wider, within the bound.
A program may use at most 64 MiB of HBM per device.

```python
import math
import jax
import jax.numpy as jnp
import numpy as np
from jax import lax

HEADS = 64
KV_HEADS = 8
HD = 128
IMG_TOK = 1601
ROWS = 256
IMG_DEV = 2
D = 8192
GROUP = 8
TEXT = 16384
IMAGES = 128
CAP = 6
N_DOCS = 64


def draw_keys(key, part):
    count = IMAGES * IMG_TOK
    base = jnp.clip(jax.random.normal(jax.random.fold_in(key, 13), (count, KV_HEADS, HD), jnp.float32), -6.0, 6.0)
    return base.reshape(count, KV_HEADS * HD).astype(jnp.bfloat16)


def draw_queries(key, part):
    base = jnp.clip(jax.random.normal(jax.random.fold_in(key, 23), (TEXT, HEADS, HD), jnp.float32), -6.0, 6.0)
    return base.reshape(TEXT, HEADS * HD).astype(jnp.bfloat16)


def draw_values(key, part):
    count = IMAGES * IMG_TOK
    head = jnp.arange(KV_HEADS).astype(jnp.float32) / (KV_HEADS - 1)
    base = jnp.clip(jax.random.normal(jax.random.fold_in(key, 32), (count, KV_HEADS, HD), jnp.float32), -5.0, 5.0)
    base = base * (0.6 * 3.0 ** head)[None, :, None]
    return base.reshape(count, KV_HEADS * HD).astype(jnp.bfloat16)


def plant(drawn, stream_key, least, top_value):
    longest = drawn.shape.index(max(drawn.shape))
    spots = []
    for shift in (0, 1):
        where = [jax.random.randint(jax.random.fold_in(stream_key, axis), (), 0, length) for axis, length in enumerate(drawn.shape)]
        where[longest] = (where[longest] + shift) % drawn.shape[longest]
        spots.append(tuple(where))
    return drawn.at[spots[0]].set(least).at[spots[1]].set(top_value)


def assign_block(rng, own, number, rows, amount, top, most, slope):
    ranking = jax.random.permutation(rng, amount)
    heavy_load, common = shares(amount, rows * top, most, slope, True), shares(amount, rows * top, most, slope, False)
    places = jnp.arange(amount)

    def named(lengths, turn):
        used = int((lengths > 0).sum())
        fixed = max(1, used // 4)
        shifted = fixed + (places - fixed + turn * (used - fixed)) % max(1, amount - fixed)
        return jnp.zeros((amount,), jnp.int32).at[ranking[jnp.where(places < fixed, places, shifted)]].set(jnp.asarray(lengths, jnp.int32))

    lengths = jnp.where(number % 4 == 0, named(heavy_load, number // 4), named(common, number - number // 4 - 1))
    mixed = jax.random.permutation(jax.random.fold_in(own, 3), amount)
    source_of, sink = mixed[0:amount // 2 * 2:2], mixed[1:amount // 2 * 2:2]
    slack = jnp.minimum(lengths[source_of] - 1, most - lengths[sink]) // 2
    slack = jnp.where((source_of == ranking[0]) | (sink == ranking[0]) | (lengths[sink] == 0), 0, jnp.maximum(slack, 0))
    shifted = jax.random.randint(jax.random.fold_in(own, 4), (amount // 2,), 0, 1 << 20) % (slack + 1)
    lengths = lengths.at[source_of].add(-shifted).at[sink].add(shifted)
    items = jnp.searchsorted(jnp.cumsum(lengths), jnp.arange(rows * top), side="right").astype(jnp.int32)
    table = items.reshape(top, rows).T
    table = table[jax.random.permutation(jax.random.fold_in(own, 1), rows)]
    turn = jax.random.randint(jax.random.fold_in(own, 2), (rows, 1), 0, top)
    return jnp.take_along_axis(table, (jnp.arange(top)[None, :] + turn) % top, axis=1)


def shares(count, total, limit, lean, full):
    weights = [(1 << 20) // math.isqrt(rank ** lean) + 1 for rank in range(1, count + 1)]
    largest = limit if full else min(limit, max(-(-total // count), total * weights[0] // sum(weights)))
    least = 1 if total - largest >= count - 1 else 0
    counts, surplus = [largest] + [least] * (count - 1), total - largest - least * (count - 1)
    while surplus > 0:
        free = [i for i in range(1, count) if counts[i] < largest] or [i for i in range(1, count) if counts[i] < limit]
        pool, remaining = sum([weights[i] for i in free]), surplus
        for i in free:
            more = min(limit - counts[i], max(1, remaining * weights[i] // pool), surplus)
            counts[i] = counts[i] + more
            surplus = surplus - more
    return np.array(counts)


def setup_inputs(seed: int = 0) -> dict:
    streams_of = jax.random.split(jax.random.key(seed), 7)
    queries = draw_queries(jax.random.fold_in(streams_of[6], 71), 0)
    keys = draw_keys(jax.random.fold_in(streams_of[6], 71), 0)
    values = draw_values(jax.random.fold_in(streams_of[6], 71), 0)
    owner_of_row_keys = jax.random.split(jax.random.fold_in(streams_of[3], 1), TEXT // ROWS)
    owner_of_row_turns = jax.random.permutation(jax.random.fold_in(streams_of[3], 3), TEXT // ROWS)
    owner_of_row = jax.vmap(lambda own, number: assign_block(jax.random.fold_in(streams_of[3], 2), own, number, ROWS, N_DOCS, 1, CAP, 2))(owner_of_row_keys, owner_of_row_turns).reshape((TEXT, 1))
    visible = plant(jax.random.randint(streams_of[4], (TEXT,), 1, IMG_DEV + 1), jax.random.fold_in(streams_of[4], 1), 1, IMG_DEV).astype(jnp.int32)
    gain = jnp.clip(1.0 + 0.18 * jax.random.normal(streams_of[5], (D,), jnp.float32), 0.099609375, 1.8984375).astype(jnp.bfloat16)
    return {"queries": queries, "keys": keys, "values": values, "owner_of_row": owner_of_row, "visible": visible, "gain": gain}


def reference(queries, keys, values, owner_of_row, visible, gain):
    scale = 1.0 / HD ** 0.5
    route = owner_of_row[:, 0].astype(jnp.int32)
    key_sets = keys.reshape(N_DOCS, IMG_DEV * IMG_TOK, KV_HEADS, HD)
    value_sets = values.reshape(N_DOCS, IMG_DEV * IMG_TOK, KV_HEADS, HD)
    token_image = (jnp.arange(IMG_DEV * IMG_TOK) // IMG_TOK).astype(jnp.int32)

    def per_owner(carry, owner):
        chosen = jnp.nonzero(route == owner, size=N_DOCS * CAP, fill_value=TEXT)[0].astype(jnp.int32)
        safe = jnp.minimum(chosen, TEXT - 1)
        rows_q = queries[safe].reshape(-1, KV_HEADS, GROUP, HD).astype(jnp.float32)
        seen = visible[safe].astype(jnp.int32)
        owner_keys = key_sets[owner].astype(jnp.float32)
        owner_values = value_sets[owner].astype(jnp.float32)
        scores = jnp.einsum('rkgd,tkd->rkgt', rows_q, owner_keys) * scale
        allowed = token_image[None, :] < seen[:, None]
        scores = jnp.where(allowed[:, None, None, :], scores, jnp.float32(-1e+30))
        top = lax.optimization_barrier(jnp.max(scores, axis=-1, keepdims=True))
        weights = jnp.exp(scores - top)
        total = lax.optimization_barrier(jnp.sum(weights, axis=-1))
        probs = lax.optimization_barrier(weights.astype(jnp.bfloat16)).astype(jnp.float32)
        context = jnp.einsum('rkgt,tkd->rkgd', probs, owner_values) / total[..., None]
        context = context.astype(jnp.bfloat16).reshape(-1, D)
        carry = carry.at[chosen].set(context, mode='drop')
        return (carry, None)
    start = jnp.zeros((TEXT, D), jnp.bfloat16)
    context, unused = lax.scan(per_owner, start, jnp.arange(N_DOCS, dtype=jnp.int32))
    wide = context.astype(jnp.float32)
    power = lax.optimization_barrier(jnp.sum(wide * wide, axis=-1))
    scaled = wide * lax.rsqrt(power / D + 1e-05)[:, None] * gain.astype(jnp.float32)[None, :]
    return scaled.astype(jnp.bfloat16)
```

```python
import math

import jax
import jax.numpy as jnp
from jax import lax
from jax.experimental import pallas as pl
from jax.experimental.pallas import tpu as pltpu
from jax.sharding import PartitionSpec as P

HD = 128
IMG_TOK = 1601
D = 8192
GROUP = 8


def rescale(context, power, gain):
    wide = context.astype(jnp.float32)
    factor = lax.rsqrt(power / D + 1e-05)
    return (wide * factor[..., None] * gain.astype(jnp.float32)).astype(jnp.bfloat16)


def squares(context):
    wide = context.astype(jnp.float32)
    return jnp.sum(wide * wide, axis=-1)


def attend_kernel(seen_ref, q_ref, k_ref, v_ref, o_ref):
    tm = q_ref.shape[0]
    tp = k_ref.shape[0]
    scale = 1.0 / HD**0.5
    limit = seen_ref[...] * IMG_TOK
    allowed = lax.broadcasted_iota(jnp.int32, (tm, tp), 1) < limit
    keys = k_ref[...]
    vals = v_ref[...]
    for g in range(GROUP):
        q = q_ref[:, g * HD : (g + 1) * HD]
        s = lax.dot_general(
            q, keys, (((1,), (1,)), ((), ())), preferred_element_type=jnp.float32
        ) * scale
        s = jnp.where(allowed, s, jnp.float32(-1e30))
        top = jnp.max(s, axis=1, keepdims=True)
        w = jnp.exp(s - top)
        total = jnp.sum(w, axis=1, keepdims=True)
        ctx = jnp.dot(w.astype(jnp.bfloat16), vals, preferred_element_type=jnp.float32)
        o_ref[:, g * HD : (g + 1) * HD] = (ctx / total).astype(o_ref.dtype)


def attend(q, seen, keys, values):
    rows, width = q.shape
    tokens = keys.shape[0]
    padded = -(-tokens // 128) * 128
    kv_local = keys.shape[1] // HD
    kp = jnp.pad(keys, ((0, padded - tokens), (0, 0)))
    vp = jnp.pad(values, ((0, padded - tokens), (0, 0)))
    tm = math.gcd(rows, 128)
    return pl.pallas_call(
        attend_kernel,
        grid=(kv_local, rows // tm),
        in_specs=[
            pl.BlockSpec((tm, 1), lambda k, i: (i, 0)),
            pl.BlockSpec((tm, GROUP * HD), lambda k, i: (i, k)),
            pl.BlockSpec((padded, HD), lambda k, i: (0, k)),
            pl.BlockSpec((padded, HD), lambda k, i: (0, k)),
        ],
        out_specs=pl.BlockSpec((tm, GROUP * HD), lambda k, i: (i, k)),
        out_shape=jax.ShapeDtypeStruct((rows, width), jnp.bfloat16),
    )(seen, q, kp, vp)


def shards(queries, keys, values, owner_of_row, visible, gain):
    docs = lax.axis_size("docs")
    rows = queries.shape[0]
    width = queries.shape[1]
    cap = max(2, 3 * rows // (2 * docs))
    route = owner_of_row[:, 0]
    onehot = (route[:, None] == jnp.arange(docs, dtype=jnp.int32)[None, :]).astype(jnp.int32)
    before = jnp.cumsum(onehot, axis=0) - onehot
    rank = jnp.sum(before * onehot, axis=1)
    target = route * cap + rank
    place = (jnp.arange(docs * cap, dtype=jnp.int32)[:, None] == target[None, :]).astype(
        jnp.bfloat16
    )
    packed = jnp.dot(place, queries, preferred_element_type=jnp.float32).astype(jnp.bfloat16)
    packed = packed.reshape(docs, cap, width)
    seen_packed = jnp.dot(place, visible.astype(jnp.bfloat16), preferred_element_type=jnp.float32)
    seen_packed = seen_packed.astype(jnp.bfloat16).reshape(docs, cap)
    arrived, arrived_seen = (
        lax.all_to_all(packed, "docs", split_axis=0, concat_axis=0, tiled=True),
        lax.all_to_all(seen_packed, "docs", split_axis=0, concat_axis=0, tiled=True),
    )
    context = attend(
        arrived.reshape(-1, width),
        arrived_seen.reshape(-1, 1).astype(jnp.int32),
        keys,
        values,
    ).reshape(arrived.shape)
    returned = lax.all_to_all(context, "docs", split_axis=0, concat_axis=0, tiled=True)
    flat_back = returned.reshape(docs * cap, width)
    mine = jnp.einsum("sr,sc->rc", place, flat_back, preferred_element_type=jnp.float32).astype(
        jnp.bfloat16
    )
    power = lax.psum(squares(mine), "mp")
    return rescale(mine, power, gain)


def solution(mesh):
    return jax.shard_map(
        shards,
        mesh=mesh,
        in_specs=(
            P("docs", "mp"),
            P("docs", "mp"),
            P("docs", "mp"),
            P("docs", None),
            P("docs"),
            P("mp"),
        ),
        out_specs=P("docs", "mp"),
        check_vma=False,
    )
```

```python
import math

import jax
import jax.numpy as jnp
from jax import lax
from jax.experimental import pallas as pl
from jax.experimental.pallas import tpu as pltpu
from jax.sharding import PartitionSpec as P

HD = 128
IMG_TOK = 1601
D = 8192
GROUP = 8


def rescale(context, power, gain):
    wide = context.astype(jnp.float32)
    factor = lax.rsqrt(power / D + 1e-05)
    return (wide * factor[..., None] * gain.astype(jnp.float32)).astype(jnp.bfloat16)


def squares(context):
    wide = context.astype(jnp.float32)
    return jnp.sum(wide * wide, axis=-1)


def attend_kernel(seen_ref, q_ref, k_ref, v_ref, o_ref):
    tm = q_ref.shape[0]
    tp = k_ref.shape[0]
    scale = 1.0 / HD**0.5
    limit = seen_ref[:, 0:1].astype(jnp.float32) * IMG_TOK
    allowed = lax.broadcasted_iota(jnp.int32, (tm, tp), 1).astype(jnp.float32) < limit
    keys = k_ref[...]
    vals = v_ref[...]
    for g in range(GROUP):
        q = q_ref[:, g * HD : (g + 1) * HD]
        s = lax.dot_general(
            q, keys, (((1,), (1,)), ((), ())), preferred_element_type=jnp.float32
        ) * scale
        s = jnp.where(allowed, s, jnp.float32(-1e30))
        top = jnp.max(s, axis=1, keepdims=True)
        w = jnp.exp(s - top)
        total = jnp.sum(w, axis=1, keepdims=True)
        ctx = jnp.dot(w.astype(jnp.bfloat16), vals, preferred_element_type=jnp.float32)
        o_ref[:, g * HD : (g + 1) * HD] = (ctx / total).astype(o_ref.dtype)


def attend(q, keys, values):
    rows = q.shape[0]
    width = q.shape[1] - 128
    tokens = keys.shape[0]
    padded = -(-tokens // 128) * 128
    kv_local = keys.shape[1] // HD
    kp = jnp.pad(keys, ((0, padded - tokens), (0, 0)))
    vp = jnp.pad(values, ((0, padded - tokens), (0, 0)))
    tm = math.gcd(rows, 128)
    return pl.pallas_call(
        attend_kernel,
        grid=(kv_local, rows // tm),
        in_specs=[
            pl.BlockSpec((tm, 128), lambda k, i: (i, width // 128)),
            pl.BlockSpec((tm, GROUP * HD), lambda k, i: (i, k)),
            pl.BlockSpec((padded, HD), lambda k, i: (0, k)),
            pl.BlockSpec((padded, HD), lambda k, i: (0, k)),
        ],
        out_specs=pl.BlockSpec((tm, GROUP * HD), lambda k, i: (i, k)),
        out_shape=jax.ShapeDtypeStruct((rows, width), jnp.bfloat16),
    )(q, q, kp, vp)


def shards(queries, keys, values, owner_of_row, visible, gain):
    docs = lax.axis_size("docs")
    rows = queries.shape[0]
    width = queries.shape[1]
    cap = max(2, 3 * rows // (2 * docs))
    route = owner_of_row[:, 0]
    onehot = (route[:, None] == jnp.arange(docs, dtype=jnp.int32)[None, :]).astype(jnp.int32)
    before = jnp.cumsum(onehot, axis=0) - onehot
    rank = jnp.sum(before * onehot, axis=1)
    target = route * cap + rank
    place = (jnp.arange(docs * cap, dtype=jnp.int32)[:, None] == target[None, :]).astype(
        jnp.bfloat16
    )
    extra = jnp.broadcast_to(visible.astype(jnp.bfloat16)[:, None], (rows, 128))
    payload = jnp.concatenate([queries, extra], axis=1)
    packed = jnp.dot(place, payload, preferred_element_type=jnp.float32).astype(jnp.bfloat16)
    packed = packed.reshape(docs, cap, width + 128)
    arrived = lax.all_to_all(packed, "docs", split_axis=0, concat_axis=0, tiled=True)
    context = attend(arrived.reshape(docs * cap, width + 128), keys, values)
    context = context.reshape(docs, cap, width)
    returned = lax.all_to_all(context, "docs", split_axis=0, concat_axis=0, tiled=True)
    flat_back = returned.reshape(docs * cap, width)
    mine = jnp.einsum("sr,sc->rc", place, flat_back, preferred_element_type=jnp.float32).astype(
        jnp.bfloat16
    )
    power = lax.psum(squares(mine), "mp")
    return rescale(mine, power, gain)


def solution(mesh):
    return jax.shard_map(
        shards,
        mesh=mesh,
        in_specs=(
            P("docs", "mp"),
            P("docs", "mp"),
            P("docs", "mp"),
            P("docs", None),
            P("docs"),
            P("mp"),
        ),
        out_specs=P("docs", "mp"),
        check_vma=False,
    )
```

```python
import math

import jax
import jax.numpy as jnp
from jax import lax
from jax.experimental import pallas as pl
from jax.experimental.pallas import tpu as pltpu
from jax.sharding import PartitionSpec as P

HD = 128
IMG_TOK = 1601
D = 8192
GROUP = 8


def rescale(context, power, gain):
    wide = context.astype(jnp.float32)
    factor = lax.rsqrt(power / D + 1e-05)
    return (wide * factor[..., None] * gain.astype(jnp.float32)).astype(jnp.bfloat16)


def squares(context):
    wide = context.astype(jnp.float32)
    return jnp.sum(wide * wide, axis=-1)


def attend_kernel(seen_ref, q_ref, k_ref, v_ref, o_ref):
    tm = q_ref.shape[0]
    tp = k_ref.shape[0]
    scale = 1.0 / HD**0.5
    limit = seen_ref[:, 0:1].astype(jnp.float32) * IMG_TOK
    allowed = lax.broadcasted_iota(jnp.int32, (tm, tp), 1).astype(jnp.float32) < limit
    keys = k_ref[...]
    vals = v_ref[...]
    for g in range(GROUP):
        q = q_ref[:, g * HD : (g + 1) * HD]
        s = lax.dot_general(
            q, keys, (((1,), (1,)), ((), ())), preferred_element_type=jnp.float32
        ) * scale
        s = jnp.where(allowed, s, jnp.float32(-1e30))
        top = jnp.max(s, axis=1, keepdims=True)
        w = jnp.exp(s - top)
        total = jnp.sum(w, axis=1, keepdims=True)
        ctx = jnp.dot(w.astype(jnp.bfloat16), vals, preferred_element_type=jnp.float32)
        o_ref[:, g * HD : (g + 1) * HD] = (ctx / total).astype(o_ref.dtype)


def attend(q, keys, values):
    rows = q.shape[0]
    width = q.shape[1] - 128
    tokens = keys.shape[0]
    padded = -(-tokens // 128) * 128
    kv_local = keys.shape[1] // HD
    kp = jnp.pad(keys, ((0, padded - tokens), (0, 0)))
    vp = jnp.pad(values, ((0, padded - tokens), (0, 0)))
    tm = math.gcd(rows, 128)
    return pl.pallas_call(
        attend_kernel,
        grid=(kv_local, rows // tm),
        in_specs=[
            pl.BlockSpec((tm, 128), lambda k, i: (i, width // 128)),
            pl.BlockSpec((tm, GROUP * HD), lambda k, i: (i, k)),
            pl.BlockSpec((padded, HD), lambda k, i: (0, k)),
            pl.BlockSpec((padded, HD), lambda k, i: (0, k)),
        ],
        out_specs=pl.BlockSpec((tm, GROUP * HD), lambda k, i: (i, k)),
        out_shape=jax.ShapeDtypeStruct((rows, width), jnp.bfloat16),
    )(q, q, kp, vp)


def exchange_kernel(x_ref, o_ref, send_sem, recv_sem):
    me = lax.axis_index("docs")
    col = lax.axis_index("mp")
    docs = x_ref.shape[0]
    own = pltpu.make_async_copy(x_ref.at[me], o_ref.at[me], recv_sem)
    own.start()

    def send(d, carry):
        peer = lax.rem(me + d, docs)
        pltpu.make_async_remote_copy(
            src_ref=x_ref.at[peer],
            dst_ref=o_ref.at[me],
            send_sem=send_sem,
            recv_sem=recv_sem,
            device_id=(peer, col),
            device_id_type=pl.DeviceIdType.MESH,
        ).start()
        return carry

    lax.fori_loop(1, docs, send, 0)
    pltpu.make_async_copy(x_ref.at[pl.ds(1, docs - 1)], o_ref.at[pl.ds(1, docs - 1)], send_sem).wait()
    pltpu.make_async_copy(x_ref, o_ref, recv_sem).wait()


def exchange(x):
    return pl.pallas_call(
        exchange_kernel,
        in_specs=[pl.BlockSpec(memory_space=pl.ANY)],
        out_specs=pl.BlockSpec(memory_space=pl.ANY),
        out_shape=jax.ShapeDtypeStruct(x.shape, x.dtype),
        scratch_shapes=[pltpu.SemaphoreType.DMA(()), pltpu.SemaphoreType.DMA(())],
        compiler_params=pltpu.CompilerParams(has_side_effects=True),
    )(x)


def shards(queries, keys, values, owner_of_row, visible, gain):
    docs = lax.axis_size("docs")
    rows = queries.shape[0]
    width = queries.shape[1]
    cap = max(2, 3 * rows // (2 * docs))
    route = owner_of_row[:, 0]
    onehot = (route[:, None] == jnp.arange(docs, dtype=jnp.int32)[None, :]).astype(jnp.int32)
    before = jnp.cumsum(onehot, axis=0) - onehot
    rank = jnp.sum(before * onehot, axis=1)
    target = route * cap + rank
    place = (jnp.arange(docs * cap, dtype=jnp.int32)[:, None] == target[None, :]).astype(
        jnp.bfloat16
    )
    extra = jnp.broadcast_to(visible.astype(jnp.bfloat16)[:, None], (rows, 128))
    payload = jnp.concatenate([queries, extra], axis=1)
    packed = jnp.dot(place, payload, preferred_element_type=jnp.float32).astype(jnp.bfloat16)
    packed = packed.reshape(docs, cap, width + 128)
    arrived = exchange(packed)
    context = attend(arrived.reshape(docs * cap, width + 128), keys, values)
    context = context.reshape(docs, cap, width)
    returned = exchange(context)
    flat_back = returned.reshape(docs * cap, width)
    mine = jnp.einsum("sr,sc->rc", place, flat_back, preferred_element_type=jnp.float32).astype(
        jnp.bfloat16
    )
    power = lax.psum(squares(mine), "mp")
    return rescale(mine, power, gain)


def solution(mesh):
    return jax.shard_map(
        shards,
        mesh=mesh,
        in_specs=(
            P("docs", "mp"),
            P("docs", "mp"),
            P("docs", "mp"),
            P("docs", None),
            P("docs"),
            P("mp"),
        ),
        out_specs=P("docs", "mp"),
        check_vma=False,
    )
```

```python
import math

import jax
import jax.numpy as jnp
from jax import lax
from jax.experimental import pallas as pl
from jax.experimental.pallas import tpu as pltpu
from jax.sharding import PartitionSpec as P

HD = 128
IMG_TOK = 1601
D = 8192
GROUP = 8


def rescale(context, power, gain):
    wide = context.astype(jnp.float32)
    factor = lax.rsqrt(power / D + 1e-05)
    return (wide * factor[..., None] * gain.astype(jnp.float32)).astype(jnp.bfloat16)


def squares(context):
    wide = context.astype(jnp.float32)
    return jnp.sum(wide * wide, axis=-1)


def attend_kernel(seen_ref, q_ref, k_ref, v_ref, o_ref):
    tm = q_ref.shape[0]
    tp = k_ref.shape[0]
    scale = 1.0 / HD**0.5
    limit = seen_ref[...] * IMG_TOK
    allowed = lax.broadcasted_iota(jnp.int32, (tm, tp), 1).astype(jnp.float32) < limit
    keys = k_ref[...]
    vals = v_ref[...]
    for g in range(GROUP):
        q = q_ref[:, g * HD : (g + 1) * HD]
        s = lax.dot_general(
            q, keys, (((1,), (1,)), ((), ())), preferred_element_type=jnp.float32
        ) * scale
        s = jnp.where(allowed, s, jnp.float32(-1e30))
        top = jnp.max(s, axis=1, keepdims=True)
        w = jnp.exp(s - top)
        total = jnp.sum(w, axis=1, keepdims=True)
        ctx = jnp.dot(w.astype(jnp.bfloat16), vals, preferred_element_type=jnp.float32)
        o_ref[:, g * HD : (g + 1) * HD] = (ctx / total).astype(o_ref.dtype)


def attend(q, seen, keys, values):
    rows, width = q.shape
    tokens = keys.shape[0]
    padded = -(-tokens // 128) * 128
    kv_local = keys.shape[1] // HD
    kp = jnp.pad(keys, ((0, padded - tokens), (0, 0)))
    vp = jnp.pad(values, ((0, padded - tokens), (0, 0)))
    tm = math.gcd(rows, 128)
    return pl.pallas_call(
        attend_kernel,
        grid=(kv_local, rows // tm),
        in_specs=[
            pl.BlockSpec((tm, 1), lambda k, i: (i, 0)),
            pl.BlockSpec((tm, GROUP * HD), lambda k, i: (i, k)),
            pl.BlockSpec((padded, HD), lambda k, i: (0, k)),
            pl.BlockSpec((padded, HD), lambda k, i: (0, k)),
        ],
        out_specs=pl.BlockSpec((tm, GROUP * HD), lambda k, i: (i, k)),
        out_shape=jax.ShapeDtypeStruct((rows, width), jnp.bfloat16),
    )(seen, q, kp, vp)


def shards(queries, keys, values, owner_of_row, visible, gain):
    docs = lax.axis_size("docs")
    rows = queries.shape[0]
    width = queries.shape[1]
    cap = max(2, 3 * rows // (2 * docs))
    route = owner_of_row[:, 0]
    onehot = (route[:, None] == jnp.arange(docs, dtype=jnp.int32)[None, :]).astype(jnp.int32)
    before = jnp.cumsum(onehot, axis=0) - onehot
    rank = jnp.sum(before * onehot, axis=1)
    target = route * cap + rank
    place = (jnp.arange(docs * cap, dtype=jnp.int32)[:, None] == target[None, :]).astype(
        jnp.bfloat16
    )
    packed = jnp.dot(place, queries, preferred_element_type=jnp.float32).astype(jnp.bfloat16)
    seen = jnp.dot(place, visible.astype(jnp.bfloat16), preferred_element_type=jnp.float32)
    lanes = cap * width // 8
    slabs = packed.reshape(docs, 8, lanes)
    seen_tile = jnp.pad(seen.astype(jnp.bfloat16).reshape(docs, 1, cap), ((0, 0), (0, 7), (0, 128 - cap)))
    sent = jnp.concatenate([slabs, seen_tile], axis=2)
    arrived = lax.all_to_all(sent, "docs", split_axis=0, concat_axis=0, tiled=True)
    arrived_q = arrived[:, :, :lanes].reshape(docs * cap, width)
    arrived_seen = arrived[:, 0, lanes : lanes + cap].astype(jnp.float32).reshape(docs * cap, 1)
    context = attend(arrived_q, arrived_seen, keys, values)
    returned = lax.all_to_all(context.reshape(docs, 8, lanes), "docs", split_axis=0, concat_axis=0, tiled=True)
    flat_back = returned.reshape(docs * cap, width)
    mine = jnp.einsum("sr,sc->rc", place, flat_back, preferred_element_type=jnp.float32).astype(
        jnp.bfloat16
    )
    power = lax.psum(squares(mine), "mp")
    return rescale(mine, power, gain)


def solution(mesh):
    return jax.shard_map(
        shards,
        mesh=mesh,
        in_specs=(
            P("docs", "mp"),
            P("docs", "mp"),
            P("docs", "mp"),
            P("docs", None),
            P("docs"),
            P("mp"),
        ),
        out_specs=P("docs", "mp"),
        check_vma=False,
    )
```

```python
import math

import jax
import jax.numpy as jnp
from jax import lax
from jax.experimental import pallas as pl
from jax.experimental.pallas import tpu as pltpu
from jax.sharding import PartitionSpec as P

HD = 128
IMG_TOK = 1601
D = 8192
GROUP = 8


def rescale(context, power, gain):
    wide = context.astype(jnp.float32)
    factor = lax.rsqrt(power / D + 1e-05)
    return (wide * factor[..., None] * gain.astype(jnp.float32)).astype(jnp.bfloat16)


def squares(context):
    wide = context.astype(jnp.float32)
    return jnp.sum(wide * wide, axis=-1)


def attend_kernel(seen_ref, q_ref, k_ref, v_ref, o_ref):
    tm = q_ref.shape[0]
    tp = k_ref.shape[0]
    scale = 1.0 / HD**0.5
    limit = seen_ref[...] * IMG_TOK
    allowed = lax.broadcasted_iota(jnp.int32, (tm, tp), 1).astype(jnp.float32) < limit
    keys = k_ref[...]
    vals = v_ref[...]
    for g in range(GROUP):
        q = q_ref[:, g * HD : (g + 1) * HD]
        s = lax.dot_general(
            q, keys, (((1,), (1,)), ((), ())), preferred_element_type=jnp.float32
        ) * scale
        s = jnp.where(allowed, s, jnp.float32(-1e30))
        top = jnp.max(s, axis=1, keepdims=True)
        w = jnp.exp(s - top)
        total = jnp.sum(w, axis=1, keepdims=True)
        ctx = jnp.dot(w.astype(jnp.bfloat16), vals, preferred_element_type=jnp.float32)
        o_ref[:, g * HD : (g + 1) * HD] = (ctx / total).astype(o_ref.dtype)


def attend(q, seen, keys, values):
    rows, width = q.shape
    tokens = keys.shape[0]
    padded = -(-tokens // 128) * 128
    kv_local = keys.shape[1] // HD
    kp = jnp.pad(keys, ((0, padded - tokens), (0, 0)))
    vp = jnp.pad(values, ((0, padded - tokens), (0, 0)))
    tm = math.gcd(rows, 128)
    return pl.pallas_call(
        attend_kernel,
        grid=(kv_local, rows // tm),
        in_specs=[
            pl.BlockSpec((tm, 1), lambda k, i: (i, 0)),
            pl.BlockSpec((tm, GROUP * HD), lambda k, i: (i, k)),
            pl.BlockSpec((padded, HD), lambda k, i: (0, k)),
            pl.BlockSpec((padded, HD), lambda k, i: (0, k)),
        ],
        out_specs=pl.BlockSpec((tm, GROUP * HD), lambda k, i: (i, k)),
        out_shape=jax.ShapeDtypeStruct((rows, width), jnp.bfloat16),
        cost_estimate=pl.CostEstimate(
            flops=4 * rows * width * padded,
            transcendentals=rows * (width // HD) * padded,
            bytes_accessed=4 * rows * width + 4 * padded * kv_local * HD,
        ),
    )(seen, q, kp, vp)


def shards(queries, keys, values, owner_of_row, visible, gain):
    docs = lax.axis_size("docs")
    rows = queries.shape[0]
    width = queries.shape[1]
    cap = max(2, 3 * rows // (2 * docs))
    route = owner_of_row[:, 0]
    onehot = (route[:, None] == jnp.arange(docs, dtype=jnp.int32)[None, :]).astype(jnp.int32)
    before = jnp.cumsum(onehot, axis=0) - onehot
    rank = jnp.sum(before * onehot, axis=1)
    target = route * cap + rank
    place = (jnp.arange(docs * cap, dtype=jnp.int32)[:, None] == target[None, :]).astype(
        jnp.bfloat16
    )
    packed = jnp.dot(place, queries, preferred_element_type=jnp.float32).astype(jnp.bfloat16)
    seen = jnp.dot(place, visible.astype(jnp.bfloat16), preferred_element_type=jnp.float32)
    packed = packed.reshape(docs, cap, width)
    seen = seen.astype(jnp.bfloat16).reshape(docs, cap)
    half = cap // 2
    lanes = half * width // 8
    pieces = []
    for part in range(2):
        rank_rows = slice(part * half, (part + 1) * half)
        slabs = packed[:, rank_rows].reshape(docs, 8, lanes)
        seen_tile = jnp.pad(seen[:, rank_rows].reshape(docs, 1, half), ((0, 0), (0, 7), (0, 128 - half)))
        sent = jnp.concatenate([slabs, seen_tile], axis=2)
        arrived = lax.all_to_all(sent, "docs", split_axis=0, concat_axis=0, tiled=True)
        arrived_q = arrived[:, :, :lanes].reshape(docs * half, width)
        arrived_seen = arrived[:, 0, lanes : lanes + half].astype(jnp.float32).reshape(docs * half, 1)
        context = attend(arrived_q, arrived_seen, keys, values)
        back = lax.all_to_all(context.reshape(docs, 8, lanes), "docs", split_axis=0, concat_axis=0, tiled=True)
        pieces.append(back.reshape(docs, half, width))
    returned = jnp.concatenate(pieces, axis=1)
    flat_back = returned.reshape(docs * cap, width)
    mine = jnp.einsum("sr,sc->rc", place, flat_back, preferred_element_type=jnp.float32).astype(
        jnp.bfloat16
    )
    power = lax.psum(squares(mine), "mp")
    return rescale(mine, power, gain)


def solution(mesh):
    return jax.shard_map(
        shards,
        mesh=mesh,
        in_specs=(
            P("docs", "mp"),
            P("docs", "mp"),
            P("docs", "mp"),
            P("docs", None),
            P("docs"),
            P("mp"),
        ),
        out_specs=P("docs", "mp"),
        check_vma=False,
    )
```

```python
import math

import jax
import jax.numpy as jnp
from jax import lax
from jax.experimental import pallas as pl
from jax.experimental.pallas import tpu as pltpu
from jax.sharding import PartitionSpec as P

HD = 128
IMG_TOK = 1601
D = 8192
GROUP = 8


def rescale(context, power, gain):
    wide = context.astype(jnp.float32)
    factor = lax.rsqrt(power / D + 1e-05)
    return (wide * factor[..., None] * gain.astype(jnp.float32)).astype(jnp.bfloat16)


def squares(context):
    wide = context.astype(jnp.float32)
    return jnp.sum(wide * wide, axis=-1)


def attend_kernel(seen_ref, q_ref, k_ref, v_ref, o_ref):
    tm = q_ref.shape[0]
    tp = k_ref.shape[1]
    scale = 1.0 / HD**0.5
    limit = seen_ref[...] * IMG_TOK
    allowed = lax.broadcasted_iota(jnp.int32, (tm, tp), 1).astype(jnp.float32) < limit
    keys = k_ref[...]
    vals = v_ref[...]
    for g in range(GROUP):
        q = q_ref[:, g * HD : (g + 1) * HD]
        s = jnp.dot(q, keys, preferred_element_type=jnp.float32) * scale
        s = jnp.where(allowed, s, jnp.float32(-1e30))
        top = jnp.max(s, axis=1, keepdims=True)
        w = jnp.exp(s - top)
        total = jnp.sum(w, axis=1, keepdims=True)
        ctx = jnp.dot(w.astype(jnp.bfloat16), vals, preferred_element_type=jnp.float32)
        o_ref[:, g * HD : (g + 1) * HD] = (ctx / total).astype(o_ref.dtype)


def attend(q, seen, keys, values):
    rows, width = q.shape
    tokens = keys.shape[0]
    padded = -(-tokens // 128) * 128
    kv_local = keys.shape[1] // HD
    kp = jnp.pad(keys, ((0, padded - tokens), (0, 0)))
    kp = kp.reshape(padded, kv_local, HD).transpose(1, 2, 0)
    vp = jnp.pad(values, ((0, padded - tokens), (0, 0)))
    tm = math.gcd(rows, 384)
    return pl.pallas_call(
        attend_kernel,
        grid=(kv_local, rows // tm),
        in_specs=[
            pl.BlockSpec((tm, 1), lambda k, i: (i, 0)),
            pl.BlockSpec((tm, GROUP * HD), lambda k, i: (i, k)),
            pl.BlockSpec((None, HD, padded), lambda k, i: (k, 0, 0)),
            pl.BlockSpec((padded, HD), lambda k, i: (0, k)),
        ],
        out_specs=pl.BlockSpec((tm, GROUP * HD), lambda k, i: (i, k)),
        out_shape=jax.ShapeDtypeStruct((rows, width), jnp.bfloat16),
        cost_estimate=pl.CostEstimate(
            flops=4 * rows * width * padded,
            transcendentals=rows * (width // HD) * padded,
            bytes_accessed=4 * rows * width + 4 * padded * kv_local * HD,
        ),
    )(seen, q, kp, vp)


def shards(queries, keys, values, owner_of_row, visible, gain):
    docs = lax.axis_size("docs")
    rows = queries.shape[0]
    width = queries.shape[1]
    cap = max(2, 3 * rows // (2 * docs))
    route = owner_of_row[:, 0]
    onehot = (route[:, None] == jnp.arange(docs, dtype=jnp.int32)[None, :]).astype(jnp.int32)
    before = jnp.cumsum(onehot, axis=0) - onehot
    rank = jnp.sum(before * onehot, axis=1)
    target = route * cap + rank
    place = (jnp.arange(docs * cap, dtype=jnp.int32)[:, None] == target[None, :]).astype(
        jnp.bfloat16
    )
    packed = jnp.dot(place, queries, preferred_element_type=jnp.float32).astype(jnp.bfloat16)
    seen = jnp.dot(place, visible.astype(jnp.bfloat16), preferred_element_type=jnp.float32)
    lanes = cap * width // 8
    slabs = packed.reshape(docs, 8, lanes)
    seen_tile = jnp.pad(seen.astype(jnp.bfloat16).reshape(docs, 1, cap), ((0, 0), (0, 7), (0, 128 - cap)))
    sent = jnp.concatenate([slabs, seen_tile], axis=2)
    arrived = lax.all_to_all(sent, "docs", split_axis=0, concat_axis=0, tiled=True)
    arrived_q = arrived[:, :, :lanes].reshape(docs * cap, width)
    arrived_seen = arrived[:, 0, lanes : lanes + cap].astype(jnp.float32).reshape(docs * cap, 1)
    context = attend(arrived_q, arrived_seen, keys, values)
    returned = lax.all_to_all(context.reshape(docs, 8, lanes), "docs", split_axis=0, concat_axis=0, tiled=True)
    flat_back = returned.reshape(docs * cap, width)
    mine = jnp.einsum("sr,sc->rc", place, flat_back, preferred_element_type=jnp.float32).astype(
        jnp.bfloat16
    )
    power = lax.psum(squares(mine), "mp")
    return rescale(mine, power, gain)


def solution(mesh):
    return jax.shard_map(
        shards,
        mesh=mesh,
        in_specs=(
            P("docs", "mp"),
            P("docs", "mp"),
            P("docs", "mp"),
            P("docs", None),
            P("docs"),
            P("mp"),
        ),
        out_specs=P("docs", "mp"),
        check_vma=False,
    )
```

```python
import math

import jax
import jax.numpy as jnp
from jax import lax
from jax.experimental import pallas as pl
from jax.experimental.pallas import tpu as pltpu
from jax.sharding import PartitionSpec as P

HD = 128
IMG_TOK = 1601
D = 8192
GROUP = 8


def rescale(context, power, gain):
    wide = context.astype(jnp.float32)
    factor = lax.rsqrt(power / D + 1e-05)
    return (wide * factor[..., None] * gain.astype(jnp.float32)).astype(jnp.bfloat16)


def squares(context):
    wide = context.astype(jnp.float32)
    return jnp.sum(wide * wide, axis=-1)


def attend_kernel(seen_ref, q_ref, k_ref, v_ref, o_ref):
    tm = q_ref.shape[0]
    tp = k_ref.shape[1]
    scale = 1.0 / HD**0.5
    limit = seen_ref[...] * IMG_TOK
    allowed = lax.broadcasted_iota(jnp.int32, (tm, tp), 1).astype(jnp.float32) < limit
    keys = k_ref[...]
    vals = v_ref[...]
    for g in range(GROUP):
        q = q_ref[:, g * HD : (g + 1) * HD]
        s = jnp.dot(q, keys, preferred_element_type=jnp.float32) * scale
        s = jnp.where(allowed, s, jnp.float32(-1e30))
        top = jnp.max(s, axis=1, keepdims=True)
        w = jnp.exp(s - top)
        total = jnp.sum(w, axis=1, keepdims=True)
        ctx = jnp.dot(w.astype(jnp.bfloat16), vals, preferred_element_type=jnp.float32)
        o_ref[:, g * HD : (g + 1) * HD] = (ctx / total).astype(o_ref.dtype)


def attend(q, seen, keys, values):
    rows, width = q.shape
    tokens = keys.shape[0]
    padded = -(-tokens // 128) * 128
    kv_local = keys.shape[1] // HD
    kp = jnp.pad(keys, ((0, padded - tokens), (0, 0)))
    kp = kp.reshape(padded, kv_local, HD).transpose(1, 2, 0)
    vp = jnp.pad(values, ((0, padded - tokens), (0, 0)))
    tm = math.gcd(rows, 384)
    return pl.pallas_call(
        attend_kernel,
        grid=(kv_local, rows // tm),
        in_specs=[
            pl.BlockSpec((tm, 1), lambda k, i: (i, 0)),
            pl.BlockSpec((tm, GROUP * HD), lambda k, i: (i, k)),
            pl.BlockSpec((None, HD, padded), lambda k, i: (k, 0, 0)),
            pl.BlockSpec((padded, HD), lambda k, i: (0, k)),
        ],
        out_specs=pl.BlockSpec((tm, GROUP * HD), lambda k, i: (i, k)),
        out_shape=jax.ShapeDtypeStruct((rows, width), jnp.bfloat16),
        cost_estimate=pl.CostEstimate(
            flops=4 * rows * width * padded,
            transcendentals=rows * (width // HD) * padded,
            bytes_accessed=4 * rows * width + 4 * padded * kv_local * HD,
        ),
    )(seen, q, kp, vp)


def power_kernel(x_ref, o_ref, slots, send_sem, recv_sem):
    doc = lax.axis_index("docs")
    col = lax.axis_index("mp")
    n = slots.shape[0]
    mesh_id = pl.DeviceIdType.MESH
    barrier = pltpu.get_barrier_semaphore()
    for d in range(1, n):
        pl.semaphore_signal(barrier, inc=1, device_id=(doc, lax.rem(col + d, n)), device_id_type=mesh_id)
    pl.semaphore_wait(barrier, n - 1)
    slots[col] = x_ref[...]
    copies = []
    for d in range(1, n):
        copy = pltpu.make_async_remote_copy(
            src_ref=x_ref,
            dst_ref=slots.at[col],
            send_sem=send_sem.at[d - 1],
            recv_sem=recv_sem.at[d - 1],
            device_id=(doc, lax.rem(col + d, n)),
            device_id_type=mesh_id,
        )
        copy.start()
        copies.append(copy)
    for d in range(1, n):
        copies[d - 1].wait_send()
        pltpu.make_async_copy(
            x_ref, slots.at[lax.rem(col + n - d, n)], recv_sem.at[d - 1]
        ).wait()
    total = slots[0]
    for i in range(1, n):
        total = total + slots[i]
    o_ref[...] = total


def power_sum(part):
    n = lax.axis_size("mp")
    row = part.reshape(1, -1)
    return pl.pallas_call(
        power_kernel,
        in_specs=[pl.BlockSpec(memory_space=pltpu.VMEM)],
        out_specs=pl.BlockSpec(memory_space=pltpu.VMEM),
        out_shape=jax.ShapeDtypeStruct(row.shape, row.dtype),
        scratch_shapes=[
            pltpu.VMEM((n,) + row.shape, row.dtype),
            pltpu.SemaphoreType.DMA((n - 1,)),
            pltpu.SemaphoreType.DMA((n - 1,)),
        ],
        compiler_params=pltpu.CompilerParams(collective_id=0, has_side_effects=True),
    )(row).reshape(part.shape)


def shards(queries, keys, values, owner_of_row, visible, gain):
    docs = lax.axis_size("docs")
    rows = queries.shape[0]
    width = queries.shape[1]
    cap = max(2, 3 * rows // (2 * docs))
    route = owner_of_row[:, 0]
    onehot = (route[:, None] == jnp.arange(docs, dtype=jnp.int32)[None, :]).astype(jnp.int32)
    before = jnp.cumsum(onehot, axis=0) - onehot
    rank = jnp.sum(before * onehot, axis=1)
    target = route * cap + rank
    place = (jnp.arange(docs * cap, dtype=jnp.int32)[:, None] == target[None, :]).astype(
        jnp.bfloat16
    )
    packed = jnp.dot(place, queries, preferred_element_type=jnp.float32).astype(jnp.bfloat16)
    seen = jnp.dot(place, visible.astype(jnp.bfloat16), preferred_element_type=jnp.float32)
    lanes = cap * width // 8
    slabs = packed.reshape(docs, 8, lanes)
    seen_tile = jnp.pad(seen.astype(jnp.bfloat16).reshape(docs, 1, cap), ((0, 0), (0, 7), (0, 128 - cap)))
    sent = jnp.concatenate([slabs, seen_tile], axis=2)
    arrived = lax.all_to_all(sent, "docs", split_axis=0, concat_axis=0, tiled=True)
    arrived_q = arrived[:, :, :lanes].reshape(docs * cap, width)
    arrived_seen = arrived[:, 0, lanes : lanes + cap].astype(jnp.float32).reshape(docs * cap, 1)
    context = attend(arrived_q, arrived_seen, keys, values)
    returned = lax.all_to_all(context.reshape(docs, 8, lanes), "docs", split_axis=0, concat_axis=0, tiled=True)
    flat_back = returned.reshape(docs * cap, width)
    mine = jnp.einsum("sr,sc->rc", place, flat_back, preferred_element_type=jnp.float32).astype(
        jnp.bfloat16
    )
    power = power_sum(squares(mine))
    return rescale(mine, power, gain)


def solution(mesh):
    return jax.shard_map(
        shards,
        mesh=mesh,
        in_specs=(
            P("docs", "mp"),
            P("docs", "mp"),
            P("docs", "mp"),
            P("docs", None),
            P("docs"),
            P("mp"),
        ),
        out_specs=P("docs", "mp"),
        check_vma=False,
    )
```

```python
import math

import jax
import jax.numpy as jnp
from jax import lax
from jax.experimental import pallas as pl
from jax.experimental.pallas import tpu as pltpu
from jax.sharding import PartitionSpec as P

HD = 128
IMG_TOK = 1601
D = 8192
GROUP = 8


def rescale(context, power, gain):
    wide = context.astype(jnp.float32)
    factor = lax.rsqrt(power / D + 1e-05)
    return (wide * factor[..., None] * gain.astype(jnp.float32)).astype(jnp.bfloat16)


def squares(context):
    wide = context.astype(jnp.float32)
    return jnp.sum(wide * wide, axis=-1)


def attend_kernel(seen_ref, q_ref, k_ref, v_ref, o_ref):
    tm = q_ref.shape[0]
    tp = k_ref.shape[1]
    scale = 1.0 / HD**0.5
    limit = seen_ref[...] * IMG_TOK
    allowed = lax.broadcasted_iota(jnp.int32, (tm, tp), 1).astype(jnp.float32) < limit
    bias = jnp.where(allowed, jnp.float32(0), jnp.float32(-1e30))
    keys = k_ref[...]
    vals = v_ref[...]
    for g in range(GROUP):
        q = q_ref[:, g * HD : (g + 1) * HD]
        s = jnp.dot(q, keys, preferred_element_type=jnp.float32) * scale + bias
        top = jnp.max(s, axis=1, keepdims=True)
        w = jnp.exp(s - top)
        both = jnp.dot(w.astype(jnp.bfloat16), vals, preferred_element_type=jnp.float32)
        ctx = both[:, :HD] / both[:, HD : HD + 1]
        o_ref[:, g * HD : (g + 1) * HD] = ctx.astype(o_ref.dtype)


def attend(q, seen, keys, values):
    rows, width = q.shape
    tokens = keys.shape[0]
    padded = -(-tokens // 128) * 128
    kv_local = keys.shape[1] // HD
    kp = jnp.pad(keys, ((0, padded - tokens), (0, 0)))
    kp = kp.reshape(padded, kv_local, HD).transpose(1, 2, 0)
    vp = jnp.pad(values, ((0, padded - tokens), (0, 0)))
    vp = vp.reshape(padded, kv_local, HD).transpose(1, 0, 2)
    ones = jnp.zeros((kv_local, padded, HD), vp.dtype).at[:, :, 0].set(1)
    vp = jnp.concatenate([vp, ones], axis=2)
    tm = math.gcd(rows, 384)
    return pl.pallas_call(
        attend_kernel,
        grid=(kv_local, rows // tm),
        in_specs=[
            pl.BlockSpec((tm, 1), lambda k, i: (i, 0)),
            pl.BlockSpec((tm, GROUP * HD), lambda k, i: (i, k)),
            pl.BlockSpec((None, HD, padded), lambda k, i: (k, 0, 0)),
            pl.BlockSpec((None, padded, 2 * HD), lambda k, i: (k, 0, 0)),
        ],
        out_specs=pl.BlockSpec((tm, GROUP * HD), lambda k, i: (i, k)),
        out_shape=jax.ShapeDtypeStruct((rows, width), jnp.bfloat16),
        cost_estimate=pl.CostEstimate(
            flops=4 * rows * width * padded,
            transcendentals=rows * (width // HD) * padded,
            bytes_accessed=4 * rows * width + 4 * padded * kv_local * HD,
        ),
    )(seen, q, kp, vp)


def power_kernel(x_ref, o_ref, slots, send_sem, recv_sem):
    doc = lax.axis_index("docs")
    col = lax.axis_index("mp")
    n = slots.shape[0]
    mesh_id = pl.DeviceIdType.MESH
    barrier = pltpu.get_barrier_semaphore()
    for d in range(1, n):
        pl.semaphore_signal(barrier, inc=1, device_id=(doc, lax.rem(col + d, n)), device_id_type=mesh_id)
    pl.semaphore_wait(barrier, n - 1)
    slots[col] = x_ref[...]
    copies = []
    for d in range(1, n):
        copy = pltpu.make_async_remote_copy(
            src_ref=x_ref,
            dst_ref=slots.at[col],
            send_sem=send_sem.at[d - 1],
            recv_sem=recv_sem.at[d - 1],
            device_id=(doc, lax.rem(col + d, n)),
            device_id_type=mesh_id,
        )
        copy.start()
        copies.append(copy)
    for d in range(1, n):
        copies[d - 1].wait_send()
        pltpu.make_async_copy(
            x_ref, slots.at[lax.rem(col + n - d, n)], recv_sem.at[d - 1]
        ).wait()
    total = slots[0]
    for i in range(1, n):
        total = total + slots[i]
    o_ref[...] = total


def power_sum(part):
    n = lax.axis_size("mp")
    row = part.reshape(1, -1)
    return pl.pallas_call(
        power_kernel,
        in_specs=[pl.BlockSpec(memory_space=pltpu.VMEM)],
        out_specs=pl.BlockSpec(memory_space=pltpu.VMEM),
        out_shape=jax.ShapeDtypeStruct(row.shape, row.dtype),
        scratch_shapes=[
            pltpu.VMEM((n,) + row.shape, row.dtype),
            pltpu.SemaphoreType.DMA((n - 1,)),
            pltpu.SemaphoreType.DMA((n - 1,)),
        ],
        compiler_params=pltpu.CompilerParams(collective_id=0, has_side_effects=True),
    )(row).reshape(part.shape)


def shards(queries, keys, values, owner_of_row, visible, gain):
    docs = lax.axis_size("docs")
    rows = queries.shape[0]
    width = queries.shape[1]
    cap = max(2, 3 * rows // (2 * docs))
    route = owner_of_row[:, 0]
    onehot = (route[:, None] == jnp.arange(docs, dtype=jnp.int32)[None, :]).astype(jnp.int32)
    before = jnp.cumsum(onehot, axis=0) - onehot
    rank = jnp.sum(before * onehot, axis=1)
    target = route * cap + rank
    place = (jnp.arange(docs * cap, dtype=jnp.int32)[:, None] == target[None, :]).astype(
        jnp.bfloat16
    )
    packed = jnp.dot(place, queries, preferred_element_type=jnp.float32).astype(jnp.bfloat16)
    seen = jnp.dot(place, visible.astype(jnp.bfloat16), preferred_element_type=jnp.float32)
    lanes = cap * width // 8
    slabs = packed.reshape(docs, 8, lanes)
    seen_tile = jnp.pad(seen.astype(jnp.bfloat16).reshape(docs, 1, cap), ((0, 0), (0, 7), (0, 128 - cap)))
    sent = jnp.concatenate([slabs, seen_tile], axis=2)
    arrived = lax.all_to_all(sent, "docs", split_axis=0, concat_axis=0, tiled=True)
    arrived_q = arrived[:, :, :lanes].reshape(docs * cap, width)
    arrived_seen = arrived[:, 0, lanes : lanes + cap].astype(jnp.float32).reshape(docs * cap, 1)
    context = attend(arrived_q, arrived_seen, keys, values)
    returned = lax.all_to_all(context.reshape(docs, 8, lanes), "docs", split_axis=0, concat_axis=0, tiled=True)
    flat_back = returned.reshape(docs * cap, width)
    mine = jnp.einsum("sr,sc->rc", place, flat_back, preferred_element_type=jnp.float32).astype(
        jnp.bfloat16
    )
    power = power_sum(squares(mine))
    return rescale(mine, power, gain)


def solution(mesh):
    return jax.shard_map(
        shards,
        mesh=mesh,
        in_specs=(
            P("docs", "mp"),
            P("docs", "mp"),
            P("docs", "mp"),
            P("docs", None),
            P("docs"),
            P("mp"),
        ),
        out_specs=P("docs", "mp"),
        check_vma=False,
    )
```

```python
import math

import jax
import jax.numpy as jnp
from jax import lax
from jax.experimental import pallas as pl
from jax.experimental.pallas import tpu as pltpu
from jax.sharding import PartitionSpec as P

HD = 128
IMG_TOK = 1601
D = 8192
GROUP = 8


def rescale(context, power, gain):
    wide = context.astype(jnp.float32)
    factor = lax.rsqrt(power / D + 1e-05)
    return (wide * factor[..., None] * gain.astype(jnp.float32)).astype(jnp.bfloat16)


def squares(context):
    wide = context.astype(jnp.float32)
    return jnp.sum(wide * wide, axis=-1)


def attend_kernel(seen_ref, q_ref, k_ref, v_ref, o_ref):
    tm = q_ref.shape[0]
    tp = k_ref.shape[1]
    scale = 1.0 / HD**0.5
    limit = seen_ref[...] * IMG_TOK
    allowed = lax.broadcasted_iota(jnp.int32, (tm, tp), 1).astype(jnp.float32) < limit
    bias = jnp.where(allowed, jnp.float32(0), jnp.float32(-1e30))
    keys = k_ref[...]
    vals = v_ref[...]
    for pair in range(0, GROUP, 4):
        scores = []
        for g in range(pair, pair + 4):
            q = q_ref[:, g * HD : (g + 1) * HD]
            scores.append(jnp.dot(q, keys, preferred_element_type=jnp.float32) * scale + bias)
        for g, s in zip(range(pair, pair + 4), scores):
            top = jnp.max(s, axis=1, keepdims=True)
            w = jnp.exp(s - top)
            both = jnp.dot(w.astype(jnp.bfloat16), vals, preferred_element_type=jnp.float32)
            ctx = both[:, :HD] / both[:, HD : HD + 1]
            o_ref[:, g * HD : (g + 1) * HD] = ctx.astype(o_ref.dtype)


def attend(q, seen, keys, values):
    rows, width = q.shape
    tokens = keys.shape[0]
    padded = -(-tokens // 128) * 128
    kv_local = keys.shape[1] // HD
    kp = jnp.pad(keys, ((0, padded - tokens), (0, 0)))
    kp = kp.reshape(padded, kv_local, HD).transpose(1, 2, 0)
    vp = jnp.pad(values, ((0, padded - tokens), (0, 0)))
    vp = vp.reshape(padded, kv_local, HD).transpose(1, 0, 2)
    ones = jnp.zeros((kv_local, padded, HD), vp.dtype).at[:, :, 0].set(1)
    vp = jnp.concatenate([vp, ones], axis=2)
    tm = math.gcd(rows, 384)
    return pl.pallas_call(
        attend_kernel,
        grid=(kv_local, rows // tm),
        in_specs=[
            pl.BlockSpec((tm, 1), lambda k, i: (i, 0)),
            pl.BlockSpec((tm, GROUP * HD), lambda k, i: (i, k)),
            pl.BlockSpec((None, HD, padded), lambda k, i: (k, 0, 0)),
            pl.BlockSpec((None, padded, 2 * HD), lambda k, i: (k, 0, 0)),
        ],
        out_specs=pl.BlockSpec((tm, GROUP * HD), lambda k, i: (i, k)),
        out_shape=jax.ShapeDtypeStruct((rows, width), jnp.bfloat16),
        cost_estimate=pl.CostEstimate(
            flops=4 * rows * width * padded,
            transcendentals=rows * (width // HD) * padded,
            bytes_accessed=4 * rows * width + 4 * padded * kv_local * HD,
        ),
    )(seen, q, kp, vp)


def power_kernel(x_ref, o_ref, slots, send_sem, recv_sem):
    doc = lax.axis_index("docs")
    col = lax.axis_index("mp")
    n = slots.shape[0]
    mesh_id = pl.DeviceIdType.MESH
    barrier = pltpu.get_barrier_semaphore()
    for d in range(1, n):
        pl.semaphore_signal(barrier, inc=1, device_id=(doc, lax.rem(col + d, n)), device_id_type=mesh_id)
    pl.semaphore_wait(barrier, n - 1)
    slots[col] = x_ref[...]
    copies = []
    for d in range(1, n):
        copy = pltpu.make_async_remote_copy(
            src_ref=x_ref,
            dst_ref=slots.at[col],
            send_sem=send_sem.at[d - 1],
            recv_sem=recv_sem.at[d - 1],
            device_id=(doc, lax.rem(col + d, n)),
            device_id_type=mesh_id,
        )
        copy.start()
        copies.append(copy)
    for d in range(1, n):
        copies[d - 1].wait_send()
        pltpu.make_async_copy(
            x_ref, slots.at[lax.rem(col + n - d, n)], recv_sem.at[d - 1]
        ).wait()
    total = slots[0]
    for i in range(1, n):
        total = total + slots[i]
    o_ref[...] = total


def power_sum(part):
    n = lax.axis_size("mp")
    row = part.reshape(1, -1)
    return pl.pallas_call(
        power_kernel,
        in_specs=[pl.BlockSpec(memory_space=pltpu.VMEM)],
        out_specs=pl.BlockSpec(memory_space=pltpu.VMEM),
        out_shape=jax.ShapeDtypeStruct(row.shape, row.dtype),
        scratch_shapes=[
            pltpu.VMEM((n,) + row.shape, row.dtype),
            pltpu.SemaphoreType.DMA((n - 1,)),
            pltpu.SemaphoreType.DMA((n - 1,)),
        ],
        compiler_params=pltpu.CompilerParams(collective_id=0, has_side_effects=True),
    )(row).reshape(part.shape)


def shards(queries, keys, values, owner_of_row, visible, gain):
    docs = lax.axis_size("docs")
    rows = queries.shape[0]
    width = queries.shape[1]
    cap = max(2, 3 * rows // (2 * docs))
    route = owner_of_row[:, 0]
    onehot = (route[:, None] == jnp.arange(docs, dtype=jnp.int32)[None, :]).astype(jnp.int32)
    before = jnp.cumsum(onehot, axis=0) - onehot
    rank = jnp.sum(before * onehot, axis=1)
    target = route * cap + rank
    place = (jnp.arange(docs * cap, dtype=jnp.int32)[:, None] == target[None, :]).astype(
        jnp.bfloat16
    )
    packed = jnp.dot(place, queries, preferred_element_type=jnp.float32).astype(jnp.bfloat16)
    seen = jnp.dot(place, visible.astype(jnp.bfloat16), preferred_element_type=jnp.float32)
    lanes = cap * width // 8
    slabs = packed.reshape(docs, 8, lanes)
    seen_tile = jnp.pad(seen.astype(jnp.bfloat16).reshape(docs, 1, cap), ((0, 0), (0, 7), (0, 128 - cap)))
    sent = jnp.concatenate([slabs, seen_tile], axis=2)
    arrived = lax.all_to_all(sent, "docs", split_axis=0, concat_axis=0, tiled=True)
    arrived_q = arrived[:, :, :lanes].reshape(docs * cap, width)
    arrived_seen = arrived[:, 0, lanes : lanes + cap].astype(jnp.float32).reshape(docs * cap, 1)
    context = attend(arrived_q, arrived_seen, keys, values)
    returned = lax.all_to_all(context.reshape(docs, 8, lanes), "docs", split_axis=0, concat_axis=0, tiled=True)
    flat_back = returned.reshape(docs * cap, width)
    mine = jnp.einsum("sr,sc->rc", place, flat_back, preferred_element_type=jnp.float32).astype(
        jnp.bfloat16
    )
    power = power_sum(squares(mine))
    return rescale(mine, power, gain)


def solution(mesh):
    return jax.shard_map(
        shards,
        mesh=mesh,
        in_specs=(
            P("docs", "mp"),
            P("docs", "mp"),
            P("docs", "mp"),
            P("docs", None),
            P("docs"),
            P("mp"),
        ),
        out_specs=P("docs", "mp"),
        check_vma=False,
    )
```

```python
import math

import jax
import jax.numpy as jnp
from jax import lax
from jax.experimental import pallas as pl
from jax.experimental.pallas import tpu as pltpu
from jax.sharding import PartitionSpec as P

HD = 128
IMG_TOK = 1601
D = 8192
GROUP = 8


def rescale(context, power, gain):
    wide = context.astype(jnp.float32)
    factor = lax.rsqrt(power / D + 1e-05)
    return (wide * factor[..., None] * gain.astype(jnp.float32)).astype(jnp.bfloat16)


def squares(context):
    wide = context.astype(jnp.float32)
    return jnp.sum(wide * wide, axis=-1)


def attend_kernel(seen_ref, q_ref, k_ref, v_ref, o_ref):
    tm = q_ref.shape[0]
    tp = k_ref.shape[1]
    scale = 1.0 / HD**0.5
    limit = seen_ref[...] * IMG_TOK
    allowed = lax.broadcasted_iota(jnp.int32, (tm, tp), 1).astype(jnp.float32) < limit
    bias = jnp.where(allowed, jnp.float32(0), jnp.float32(-1e30))
    keys = k_ref[...]
    vals = v_ref[...]
    def batch(b, carry):
        scores = []
        for j in range(4):
            col = pl.multiple_of((b * 4 + j) * HD, HD)
            q = q_ref[:, pl.ds(col, HD)]
            scores.append(jnp.dot(q, keys, preferred_element_type=jnp.float32) * scale + bias)
        for j, s in enumerate(scores):
            col = pl.multiple_of((b * 4 + j) * HD, HD)
            top = jnp.max(s, axis=1, keepdims=True)
            w = jnp.exp(s - top)
            both = jnp.dot(w.astype(jnp.bfloat16), vals, preferred_element_type=jnp.float32)
            ctx = both[:, :HD] / both[:, HD : HD + 1]
            o_ref[:, pl.ds(col, HD)] = ctx.astype(o_ref.dtype)
        return carry

    lax.fori_loop(0, GROUP // 4, batch, 0)


def attend(q, seen, keys, values):
    rows, width = q.shape
    tokens = keys.shape[0]
    padded = -(-tokens // 128) * 128
    kv_local = keys.shape[1] // HD
    kp = jnp.pad(keys, ((0, padded - tokens), (0, 0)))
    kp = kp.reshape(padded, kv_local, HD).transpose(1, 2, 0)
    vp = jnp.pad(values, ((0, padded - tokens), (0, 0)))
    vp = vp.reshape(padded, kv_local, HD).transpose(1, 0, 2)
    ones = jnp.zeros((kv_local, padded, HD), vp.dtype).at[:, :, 0].set(1)
    vp = jnp.concatenate([vp, ones], axis=2)
    tm = math.gcd(rows, 384)
    return pl.pallas_call(
        attend_kernel,
        grid=(kv_local, rows // tm),
        in_specs=[
            pl.BlockSpec((tm, 1), lambda k, i: (i, 0)),
            pl.BlockSpec((tm, GROUP * HD), lambda k, i: (i, k)),
            pl.BlockSpec((None, HD, padded), lambda k, i: (k, 0, 0)),
            pl.BlockSpec((None, padded, 2 * HD), lambda k, i: (k, 0, 0)),
        ],
        out_specs=pl.BlockSpec((tm, GROUP * HD), lambda k, i: (i, k)),
        out_shape=jax.ShapeDtypeStruct((rows, width), jnp.bfloat16),
        cost_estimate=pl.CostEstimate(
            flops=4 * rows * width * padded,
            transcendentals=rows * (width // HD) * padded,
            bytes_accessed=4 * rows * width + 4 * padded * kv_local * HD,
        ),
    )(seen, q, kp, vp)


def power_kernel(x_ref, o_ref, slots, send_sem, recv_sem):
    doc = lax.axis_index("docs")
    col = lax.axis_index("mp")
    n = slots.shape[0]
    mesh_id = pl.DeviceIdType.MESH
    barrier = pltpu.get_barrier_semaphore()
    for d in range(1, n):
        pl.semaphore_signal(barrier, inc=1, device_id=(doc, lax.rem(col + d, n)), device_id_type=mesh_id)
    pl.semaphore_wait(barrier, n - 1)
    slots[col] = x_ref[...]
    copies = []
    for d in range(1, n):
        copy = pltpu.make_async_remote_copy(
            src_ref=x_ref,
            dst_ref=slots.at[col],
            send_sem=send_sem.at[d - 1],
            recv_sem=recv_sem.at[d - 1],
            device_id=(doc, lax.rem(col + d, n)),
            device_id_type=mesh_id,
        )
        copy.start()
        copies.append(copy)
    for d in range(1, n):
        copies[d - 1].wait_send()
        pltpu.make_async_copy(
            x_ref, slots.at[lax.rem(col + n - d, n)], recv_sem.at[d - 1]
        ).wait()
    total = slots[0]
    for i in range(1, n):
        total = total + slots[i]
    o_ref[...] = total


def power_sum(part):
    n = lax.axis_size("mp")
    row = part.reshape(1, -1)
    return pl.pallas_call(
        power_kernel,
        in_specs=[pl.BlockSpec(memory_space=pltpu.VMEM)],
        out_specs=pl.BlockSpec(memory_space=pltpu.VMEM),
        out_shape=jax.ShapeDtypeStruct(row.shape, row.dtype),
        scratch_shapes=[
            pltpu.VMEM((n,) + row.shape, row.dtype),
            pltpu.SemaphoreType.DMA((n - 1,)),
            pltpu.SemaphoreType.DMA((n - 1,)),
        ],
        compiler_params=pltpu.CompilerParams(collective_id=0, has_side_effects=True),
    )(row).reshape(part.shape)


def shards(queries, keys, values, owner_of_row, visible, gain):
    docs = lax.axis_size("docs")
    rows = queries.shape[0]
    width = queries.shape[1]
    cap = max(2, 3 * rows // (2 * docs))
    route = owner_of_row[:, 0]
    onehot = (route[:, None] == jnp.arange(docs, dtype=jnp.int32)[None, :]).astype(jnp.int32)
    before = jnp.cumsum(onehot, axis=0) - onehot
    rank = jnp.sum(before * onehot, axis=1)
    target = route * cap + rank
    place = (jnp.arange(docs * cap, dtype=jnp.int32)[:, None] == target[None, :]).astype(
        jnp.bfloat16
    )
    packed = jnp.dot(place, queries, preferred_element_type=jnp.float32).astype(jnp.bfloat16)
    seen = jnp.dot(place, visible.astype(jnp.bfloat16), preferred_element_type=jnp.float32)
    lanes = cap * width // 8
    slabs = packed.reshape(docs, 8, lanes)
    seen_tile = jnp.pad(seen.astype(jnp.bfloat16).reshape(docs, 1, cap), ((0, 0), (0, 7), (0, 128 - cap)))
    sent = jnp.concatenate([slabs, seen_tile], axis=2)
    arrived = lax.all_to_all(sent, "docs", split_axis=0, concat_axis=0, tiled=True)
    arrived_q = arrived[:, :, :lanes].reshape(docs * cap, width)
    arrived_seen = arrived[:, 0, lanes : lanes + cap].astype(jnp.float32).reshape(docs * cap, 1)
    context = attend(arrived_q, arrived_seen, keys, values)
    returned = lax.all_to_all(context.reshape(docs, 8, lanes), "docs", split_axis=0, concat_axis=0, tiled=True)
    flat_back = returned.reshape(docs * cap, width)
    mine = jnp.einsum("sr,sc->rc", place, flat_back, preferred_element_type=jnp.float32).astype(
        jnp.bfloat16
    )
    power = power_sum(squares(mine))
    return rescale(mine, power, gain)


def solution(mesh):
    return jax.shard_map(
        shards,
        mesh=mesh,
        in_specs=(
            P("docs", "mp"),
            P("docs", "mp"),
            P("docs", "mp"),
            P("docs", None),
            P("docs"),
            P("mp"),
        ),
        out_specs=P("docs", "mp"),
        check_vma=False,
    )
```

```python
import math

import jax
import jax.numpy as jnp
from jax import lax
from jax.experimental import pallas as pl
from jax.experimental.pallas import tpu as pltpu
from jax.sharding import PartitionSpec as P

HD = 128
IMG_TOK = 1601
D = 8192
GROUP = 8


def rescale(context, power, gain):
    wide = context.astype(jnp.float32)
    factor = lax.rsqrt(power / D + 1e-05)
    return (wide * factor[..., None] * gain.astype(jnp.float32)).astype(jnp.bfloat16)


def squares(context):
    wide = context.astype(jnp.float32)
    return jnp.sum(wide * wide, axis=-1)


def attend_kernel(seen_ref, q_ref, k_ref, v_ref, o_ref):
    tm = q_ref.shape[0]
    tp = k_ref.shape[1]
    scale = 1.0 / HD**0.5
    limit = seen_ref[...] * IMG_TOK
    allowed = lax.broadcasted_iota(jnp.int32, (tm, tp), 1).astype(jnp.float32) < limit
    bias = jnp.where(allowed, jnp.float32(0), jnp.float32(-1e30))
    keys = k_ref[...]
    vals = v_ref[...]
    for pair in range(0, GROUP, 4):
        scores = []
        for g in range(pair, pair + 4):
            q = q_ref[:, g * HD : (g + 1) * HD]
            scores.append(jnp.dot(q, keys, preferred_element_type=jnp.float32) * scale + bias)
        for g, s in zip(range(pair, pair + 4), scores):
            top = jnp.max(s, axis=1, keepdims=True)
            w = jnp.exp(s - top)
            both = jnp.dot(w.astype(jnp.bfloat16), vals, preferred_element_type=jnp.float32)
            ctx = both[:, :HD] / both[:, HD : HD + 1]
            o_ref[:, g * HD : (g + 1) * HD] = ctx.astype(o_ref.dtype)


def attend(q, seen, keys, values):
    rows, width = q.shape
    tokens = keys.shape[0]
    padded = -(-tokens // 128) * 128
    kv_local = keys.shape[1] // HD
    kp = jnp.pad(keys, ((0, padded - tokens), (0, 0)))
    kp = kp.reshape(padded, kv_local, HD).transpose(1, 2, 0)
    vp = jnp.pad(values, ((0, padded - tokens), (0, 0)))
    vp = vp.reshape(padded, kv_local, HD).transpose(1, 0, 2)
    ones = jnp.zeros((kv_local, padded, HD), vp.dtype).at[:, :, 0].set(1)
    vp = jnp.concatenate([vp, ones], axis=2)
    tm = math.gcd(rows, 384)
    return pl.pallas_call(
        attend_kernel,
        grid=(kv_local, rows // tm),
        in_specs=[
            pl.BlockSpec((tm, 1), lambda k, i: (i, 0)),
            pl.BlockSpec((tm, GROUP * HD), lambda k, i: (i, k)),
            pl.BlockSpec((None, HD, padded), lambda k, i: (k, 0, 0)),
            pl.BlockSpec((None, padded, 2 * HD), lambda k, i: (k, 0, 0)),
        ],
        out_specs=pl.BlockSpec((tm, GROUP * HD), lambda k, i: (i, k)),
        out_shape=jax.ShapeDtypeStruct((rows, width), jnp.bfloat16),
        cost_estimate=pl.CostEstimate(
            flops=4 * rows * width * padded,
            transcendentals=rows * (width // HD) * padded,
            bytes_accessed=4 * rows * width + 4 * padded * kv_local * HD,
        ),
    )(seen, q, kp, vp)


def power_kernel(x_ref, o_ref, slots, send_sem, recv_sem):
    doc = lax.axis_index("docs")
    col = lax.axis_index("mp")
    n = slots.shape[0]
    mesh_id = pl.DeviceIdType.MESH
    barrier = pltpu.get_barrier_semaphore()
    for d in range(1, n):
        pl.semaphore_signal(barrier, inc=1, device_id=(doc, lax.rem(col + d, n)), device_id_type=mesh_id)
    pl.semaphore_wait(barrier, n - 1)
    slots[col] = x_ref[...]
    copies = []
    for d in range(1, n):
        copy = pltpu.make_async_remote_copy(
            src_ref=x_ref,
            dst_ref=slots.at[col],
            send_sem=send_sem.at[d - 1],
            recv_sem=recv_sem.at[d - 1],
            device_id=(doc, lax.rem(col + d, n)),
            device_id_type=mesh_id,
        )
        copy.start()
        copies.append(copy)
    for d in range(1, n):
        copies[d - 1].wait_send()
        pltpu.make_async_copy(
            x_ref, slots.at[lax.rem(col + n - d, n)], recv_sem.at[d - 1]
        ).wait()
    total = slots[0]
    for i in range(1, n):
        total = total + slots[i]
    o_ref[...] = total


def power_sum(part):
    n = lax.axis_size("mp")
    row = part.reshape(1, -1)
    return pl.pallas_call(
        power_kernel,
        in_specs=[pl.BlockSpec(memory_space=pltpu.VMEM)],
        out_specs=pl.BlockSpec(memory_space=pltpu.VMEM),
        out_shape=jax.ShapeDtypeStruct(row.shape, row.dtype),
        scratch_shapes=[
            pltpu.VMEM((n,) + row.shape, row.dtype),
            pltpu.SemaphoreType.DMA((n - 1,)),
            pltpu.SemaphoreType.DMA((n - 1,)),
        ],
        compiler_params=pltpu.CompilerParams(collective_id=0, has_side_effects=True),
    )(row).reshape(part.shape)


def to_slabs(x, docs, cap):
    width = x.shape[1]
    lanes = cap * width // 8
    x3 = x.reshape(docs, cap, width)
    tail = x3[:, :, lanes:].reshape(docs, 8 - cap, lanes)
    return jnp.concatenate([x3[:, :, :lanes], tail], axis=1)


def from_slabs(y, cap, width):
    docs, _, lanes = y.shape
    tail = y[:, cap:, :].reshape(docs, cap, width - lanes)
    return jnp.concatenate([y[:, :cap, :], tail], axis=2).reshape(docs * cap, width)


def shards(queries, keys, values, owner_of_row, visible, gain):
    docs = lax.axis_size("docs")
    rows = queries.shape[0]
    width = queries.shape[1]
    cap = max(2, 3 * rows // (2 * docs))
    route = owner_of_row[:, 0]
    onehot = (route[:, None] == jnp.arange(docs, dtype=jnp.int32)[None, :]).astype(jnp.int32)
    before = jnp.cumsum(onehot, axis=0) - onehot
    rank = jnp.sum(before * onehot, axis=1)
    target = route * cap + rank
    place = (jnp.arange(docs * cap, dtype=jnp.int32)[:, None] == target[None, :]).astype(
        jnp.bfloat16
    )
    packed = jnp.dot(place, queries, preferred_element_type=jnp.float32).astype(jnp.bfloat16)
    seen = jnp.dot(place, visible.astype(jnp.bfloat16), preferred_element_type=jnp.float32)
    lanes = cap * width // 8
    slabs = to_slabs(packed, docs, cap)
    seen_tile = jnp.pad(seen.astype(jnp.bfloat16).reshape(docs, 1, cap), ((0, 0), (0, 7), (0, 128 - cap)))
    sent = jnp.concatenate([slabs, seen_tile], axis=2)
    arrived = lax.all_to_all(sent, "docs", split_axis=0, concat_axis=0, tiled=True)
    arrived_q = from_slabs(arrived[:, :, :lanes], cap, width)
    arrived_seen = arrived[:, 0, lanes : lanes + cap].astype(jnp.float32).reshape(docs * cap, 1)
    context = attend(arrived_q, arrived_seen, keys, values)
    returned = lax.all_to_all(to_slabs(context, docs, cap), "docs", split_axis=0, concat_axis=0, tiled=True)
    flat_back = from_slabs(returned, cap, width)
    mine = jnp.einsum("sr,sc->rc", place, flat_back, preferred_element_type=jnp.float32).astype(
        jnp.bfloat16
    )
    power = power_sum(squares(mine))
    return rescale(mine, power, gain)


def solution(mesh):
    return jax.shard_map(
        shards,
        mesh=mesh,
        in_specs=(
            P("docs", "mp"),
            P("docs", "mp"),
            P("docs", "mp"),
            P("docs", None),
            P("docs"),
            P("mp"),
        ),
        out_specs=P("docs", "mp"),
        check_vma=False,
    )
```

```python
import math

import jax
import jax.numpy as jnp
from jax import lax
from jax.experimental import pallas as pl
from jax.experimental.pallas import tpu as pltpu
from jax.sharding import PartitionSpec as P

HD = 128
IMG_TOK = 1601
D = 8192
GROUP = 8


def rescale(context, power, gain):
    wide = context.astype(jnp.float32)
    factor = lax.rsqrt(power / D + 1e-05)
    return (wide * factor[..., None] * gain.astype(jnp.float32)).astype(jnp.bfloat16)


def squares(context):
    wide = context.astype(jnp.float32)
    return jnp.sum(wide * wide, axis=-1)


def attend_kernel(seen_ref, q_ref, k_ref, v_ref, o_ref, bias_ref):
    tm = q_ref.shape[0]
    tp = k_ref.shape[1]
    scale = 1.0 / HD**0.5

    @pl.when(pl.program_id(1) == 0)
    def _():
        limit = seen_ref[...] * IMG_TOK
        allowed = lax.broadcasted_iota(jnp.int32, (tm, tp), 1).astype(jnp.float32) < limit
        bias_ref[...] = jnp.where(allowed, jnp.float32(0), jnp.float32(-1e30))

    bias = bias_ref[...]
    keys = k_ref[...]
    vals = v_ref[...]
    for pair in range(0, GROUP, 4):
        scores = []
        for g in range(pair, pair + 4):
            q = q_ref[:, g * HD : (g + 1) * HD]
            scores.append(jnp.dot(q, keys, preferred_element_type=jnp.float32) * scale + bias)
        for g, s in zip(range(pair, pair + 4), scores):
            top = jnp.max(s, axis=1, keepdims=True)
            w = jnp.exp(s - top)
            both = jnp.dot(w.astype(jnp.bfloat16), vals, preferred_element_type=jnp.float32)
            ctx = both[:, :HD] / both[:, HD : HD + 1]
            o_ref[:, g * HD : (g + 1) * HD] = ctx.astype(o_ref.dtype)


def attend(q, seen, keys, values):
    rows, width = q.shape
    tokens = keys.shape[0]
    padded = -(-tokens // 128) * 128
    kv_local = keys.shape[1] // HD
    kp = jnp.pad(keys, ((0, padded - tokens), (0, 0)))
    kp = kp.reshape(padded, kv_local, HD).transpose(1, 2, 0)
    vp = jnp.pad(values, ((0, padded - tokens), (0, 0)))
    vp = vp.reshape(padded, kv_local, HD).transpose(1, 0, 2)
    ones = jnp.zeros((kv_local, padded, HD), vp.dtype).at[:, :, 0].set(1)
    vp = jnp.concatenate([vp, ones], axis=2)
    tm = math.gcd(rows, 384)
    return pl.pallas_call(
        attend_kernel,
        grid=(rows // tm, kv_local),
        in_specs=[
            pl.BlockSpec((tm, 1), lambda i, k: (i, 0)),
            pl.BlockSpec((tm, GROUP * HD), lambda i, k: (i, k)),
            pl.BlockSpec((None, HD, padded), lambda i, k: (k, 0, 0)),
            pl.BlockSpec((None, padded, 2 * HD), lambda i, k: (k, 0, 0)),
        ],
        out_specs=pl.BlockSpec((tm, GROUP * HD), lambda i, k: (i, k)),
        scratch_shapes=[pltpu.VMEM((tm, padded), jnp.float32)],
        out_shape=jax.ShapeDtypeStruct((rows, width), jnp.bfloat16),
        cost_estimate=pl.CostEstimate(
            flops=4 * rows * width * padded,
            transcendentals=rows * (width // HD) * padded,
            bytes_accessed=4 * rows * width + 4 * padded * kv_local * HD,
        ),
    )(seen, q, kp, vp)


def power_kernel(x_ref, o_ref, slots, send_sem, recv_sem):
    doc = lax.axis_index("docs")
    col = lax.axis_index("mp")
    n = slots.shape[0]
    mesh_id = pl.DeviceIdType.MESH
    barrier = pltpu.get_barrier_semaphore()
    for d in range(1, n):
        pl.semaphore_signal(barrier, inc=1, device_id=(doc, lax.rem(col + d, n)), device_id_type=mesh_id)
    pl.semaphore_wait(barrier, n - 1)
    slots[col] = x_ref[...]
    copies = []
    for d in range(1, n):
        copy = pltpu.make_async_remote_copy(
            src_ref=x_ref,
            dst_ref=slots.at[col],
            send_sem=send_sem.at[d - 1],
            recv_sem=recv_sem.at[d - 1],
            device_id=(doc, lax.rem(col + d, n)),
            device_id_type=mesh_id,
        )
        copy.start()
        copies.append(copy)
    for d in range(1, n):
        copies[d - 1].wait_send()
        pltpu.make_async_copy(
            x_ref, slots.at[lax.rem(col + n - d, n)], recv_sem.at[d - 1]
        ).wait()
    total = slots[0]
    for i in range(1, n):
        total = total + slots[i]
    o_ref[...] = total


def power_sum(part):
    n = lax.axis_size("mp")
    row = part.reshape(1, -1)
    return pl.pallas_call(
        power_kernel,
        in_specs=[pl.BlockSpec(memory_space=pltpu.VMEM)],
        out_specs=pl.BlockSpec(memory_space=pltpu.VMEM),
        out_shape=jax.ShapeDtypeStruct(row.shape, row.dtype),
        scratch_shapes=[
            pltpu.VMEM((n,) + row.shape, row.dtype),
            pltpu.SemaphoreType.DMA((n - 1,)),
            pltpu.SemaphoreType.DMA((n - 1,)),
        ],
        compiler_params=pltpu.CompilerParams(collective_id=0, has_side_effects=True),
    )(row).reshape(part.shape)


def shards(queries, keys, values, owner_of_row, visible, gain):
    docs = lax.axis_size("docs")
    rows = queries.shape[0]
    width = queries.shape[1]
    cap = max(2, 3 * rows // (2 * docs))
    route = owner_of_row[:, 0]
    onehot = (route[:, None] == jnp.arange(docs, dtype=jnp.int32)[None, :]).astype(jnp.int32)
    before = jnp.cumsum(onehot, axis=0) - onehot
    rank = jnp.sum(before * onehot, axis=1)
    target = route * cap + rank
    place = (jnp.arange(docs * cap, dtype=jnp.int32)[:, None] == target[None, :]).astype(
        jnp.bfloat16
    )
    packed = jnp.dot(place, queries, preferred_element_type=jnp.float32).astype(jnp.bfloat16)
    seen = jnp.dot(place, visible.astype(jnp.bfloat16), preferred_element_type=jnp.float32)
    lanes = cap * width // 8
    slabs = packed.reshape(docs, 8, lanes)
    seen_tile = jnp.pad(seen.astype(jnp.bfloat16).reshape(docs, 1, cap), ((0, 0), (0, 7), (0, 128 - cap)))
    sent = jnp.concatenate([slabs, seen_tile], axis=2)
    arrived = lax.all_to_all(sent, "docs", split_axis=0, concat_axis=0, tiled=True)
    arrived_q = arrived[:, :, :lanes].reshape(docs * cap, width)
    arrived_seen = arrived[:, 0, lanes : lanes + cap].astype(jnp.float32).reshape(docs * cap, 1)
    context = attend(arrived_q, arrived_seen, keys, values)
    returned = lax.all_to_all(context.reshape(docs, 8, lanes), "docs", split_axis=0, concat_axis=0, tiled=True)
    flat_back = returned.reshape(docs * cap, width)
    mine = jnp.einsum("sr,sc->rc", place, flat_back, preferred_element_type=jnp.float32).astype(
        jnp.bfloat16
    )
    power = power_sum(squares(mine))
    return rescale(mine, power, gain)


def solution(mesh):
    return jax.shard_map(
        shards,
        mesh=mesh,
        in_specs=(
            P("docs", "mp"),
            P("docs", "mp"),
            P("docs", "mp"),
            P("docs", None),
            P("docs"),
            P("mp"),
        ),
        out_specs=P("docs", "mp"),
        check_vma=False,
    )
```

```python
import math

import jax
import jax.numpy as jnp
from jax import lax
from jax.experimental import pallas as pl
from jax.experimental.pallas import tpu as pltpu
from jax.sharding import PartitionSpec as P

HD = 128
IMG_TOK = 1601
D = 8192
GROUP = 8


def rescale(context, power, gain):
    wide = context.astype(jnp.float32)
    factor = lax.rsqrt(power / D + 1e-05)
    return (wide * factor[..., None] * gain.astype(jnp.float32)).astype(jnp.bfloat16)


def squares(context):
    wide = context.astype(jnp.float32)
    return jnp.sum(wide * wide, axis=-1)


def attend_kernel(seen_ref, q_ref, k_ref, v_ref, o_ref, bias_ref):
    tm = q_ref.shape[0]
    tp = k_ref.shape[1]
    scale = 1.0 / HD**0.5

    @pl.when(pl.program_id(1) == 0)
    def _():
        token = lax.broadcasted_iota(jnp.int32, (1, tp), 1)
        rows_of = [jnp.where(token < n * IMG_TOK, jnp.float32(0), jnp.float32(-1e30)) for n in range(3)]
        seen = seen_ref[...]
        bias_ref[...] = jnp.where(seen > 1.5, rows_of[2], jnp.where(seen > 0.5, rows_of[1], rows_of[0]))

    bias = bias_ref[...]
    keys = k_ref[...]
    vals = v_ref[...]
    for pair in range(0, GROUP, 4):
        scores = []
        for g in range(pair, pair + 4):
            q = q_ref[:, g * HD : (g + 1) * HD]
            scores.append(jnp.dot(q, keys, preferred_element_type=jnp.float32) * scale + bias)
        for g, s in zip(range(pair, pair + 4), scores):
            top = jnp.max(s, axis=1, keepdims=True)
            w = jnp.exp(s - top)
            both = jnp.dot(w.astype(jnp.bfloat16), vals, preferred_element_type=jnp.float32)
            ctx = both[:, :HD] / both[:, HD : HD + 1]
            o_ref[:, g * HD : (g + 1) * HD] = ctx.astype(o_ref.dtype)


def attend(q, seen, keys, values):
    rows, width = q.shape
    tokens = keys.shape[0]
    padded = -(-tokens // 128) * 128
    kv_local = keys.shape[1] // HD
    kp = jnp.pad(keys, ((0, padded - tokens), (0, 0)))
    kp = kp.reshape(padded, kv_local, HD).transpose(1, 2, 0)
    vp = jnp.pad(values, ((0, padded - tokens), (0, 0)))
    vp = vp.reshape(padded, kv_local, HD).transpose(1, 0, 2)
    ones = jnp.zeros((kv_local, padded, HD), vp.dtype).at[:, :, 0].set(1)
    vp = jnp.concatenate([vp, ones], axis=2)
    tm = math.gcd(rows, 384)
    return pl.pallas_call(
        attend_kernel,
        grid=(rows // tm, kv_local),
        in_specs=[
            pl.BlockSpec((tm, 1), lambda i, k: (i, 0)),
            pl.BlockSpec((tm, GROUP * HD), lambda i, k: (i, k)),
            pl.BlockSpec((None, HD, padded), lambda i, k: (k, 0, 0)),
            pl.BlockSpec((None, padded, 2 * HD), lambda i, k: (k, 0, 0)),
        ],
        out_specs=pl.BlockSpec((tm, GROUP * HD), lambda i, k: (i, k)),
        scratch_shapes=[pltpu.VMEM((tm, padded), jnp.float32)],
        out_shape=jax.ShapeDtypeStruct((rows, width), jnp.bfloat16),
        cost_estimate=pl.CostEstimate(
            flops=4 * rows * width * padded,
            transcendentals=rows * (width // HD) * padded,
            bytes_accessed=4 * rows * width + 4 * padded * kv_local * HD,
        ),
    )(seen, q, kp, vp)


def power_kernel(x_ref, o_ref, slots, send_sem, recv_sem):
    doc = lax.axis_index("docs")
    col = lax.axis_index("mp")
    n = slots.shape[0]
    mesh_id = pl.DeviceIdType.MESH
    barrier = pltpu.get_barrier_semaphore()
    for d in range(1, n):
        pl.semaphore_signal(barrier, inc=1, device_id=(doc, lax.rem(col + d, n)), device_id_type=mesh_id)
    pl.semaphore_wait(barrier, n - 1)
    slots[col] = x_ref[...]
    copies = []
    for d in range(1, n):
        copy = pltpu.make_async_remote_copy(
            src_ref=x_ref,
            dst_ref=slots.at[col],
            send_sem=send_sem.at[d - 1],
            recv_sem=recv_sem.at[d - 1],
            device_id=(doc, lax.rem(col + d, n)),
            device_id_type=mesh_id,
        )
        copy.start()
        copies.append(copy)
    for d in range(1, n):
        copies[d - 1].wait_send()
        pltpu.make_async_copy(
            x_ref, slots.at[lax.rem(col + n - d, n)], recv_sem.at[d - 1]
        ).wait()
    total = slots[0]
    for i in range(1, n):
        total = total + slots[i]
    o_ref[...] = total


def power_sum(part):
    n = lax.axis_size("mp")
    row = part.reshape(1, -1)
    return pl.pallas_call(
        power_kernel,
        in_specs=[pl.BlockSpec(memory_space=pltpu.VMEM)],
        out_specs=pl.BlockSpec(memory_space=pltpu.VMEM),
        out_shape=jax.ShapeDtypeStruct(row.shape, row.dtype),
        scratch_shapes=[
            pltpu.VMEM((n,) + row.shape, row.dtype),
            pltpu.SemaphoreType.DMA((n - 1,)),
            pltpu.SemaphoreType.DMA((n - 1,)),
        ],
        compiler_params=pltpu.CompilerParams(collective_id=0, has_side_effects=True),
    )(row).reshape(part.shape)


def shards(queries, keys, values, owner_of_row, visible, gain):
    docs = lax.axis_size("docs")
    rows = queries.shape[0]
    width = queries.shape[1]
    cap = max(2, 3 * rows // (2 * docs))
    route = owner_of_row[:, 0]
    onehot = (route[:, None] == jnp.arange(docs, dtype=jnp.int32)[None, :]).astype(jnp.int32)
    before = jnp.cumsum(onehot, axis=0) - onehot
    rank = jnp.sum(before * onehot, axis=1)
    target = route * cap + rank
    place = (jnp.arange(docs * cap, dtype=jnp.int32)[:, None] == target[None, :]).astype(
        jnp.bfloat16
    )
    packed = jnp.dot(place, queries, preferred_element_type=jnp.float32).astype(jnp.bfloat16)
    seen = jnp.dot(place, visible.astype(jnp.bfloat16), preferred_element_type=jnp.float32)
    lanes = cap * width // 8
    slabs = packed.reshape(docs, 8, lanes)
    seen_tile = jnp.pad(seen.astype(jnp.bfloat16).reshape(docs, 1, cap), ((0, 0), (0, 7), (0, 128 - cap)))
    sent = jnp.concatenate([slabs, seen_tile], axis=2)
    arrived = lax.all_to_all(sent, "docs", split_axis=0, concat_axis=0, tiled=True)
    arrived_q = arrived[:, :, :lanes].reshape(docs * cap, width)
    arrived_seen = arrived[:, 0, lanes : lanes + cap].astype(jnp.float32).reshape(docs * cap, 1)
    context = attend(arrived_q, arrived_seen, keys, values)
    returned = lax.all_to_all(context.reshape(docs, 8, lanes), "docs", split_axis=0, concat_axis=0, tiled=True)
    flat_back = returned.reshape(docs * cap, width)
    mine = jnp.einsum("sr,sc->rc", place, flat_back, preferred_element_type=jnp.float32).astype(
        jnp.bfloat16
    )
    power = power_sum(squares(mine))
    return rescale(mine, power, gain)


def solution(mesh):
    return jax.shard_map(
        shards,
        mesh=mesh,
        in_specs=(
            P("docs", "mp"),
            P("docs", "mp"),
            P("docs", "mp"),
            P("docs", None),
            P("docs"),
            P("mp"),
        ),
        out_specs=P("docs", "mp"),
        check_vma=False,
    )
```

```python
import math

import jax
import jax.numpy as jnp
from jax import lax
from jax.experimental import pallas as pl
from jax.experimental.pallas import tpu as pltpu
from jax.sharding import PartitionSpec as P

HD = 128
IMG_TOK = 1601
D = 8192
GROUP = 8


def rescale(context, power, gain):
    wide = context.astype(jnp.float32)
    factor = lax.rsqrt(power / D + 1e-05)
    return (wide * factor[..., None] * gain.astype(jnp.float32)).astype(jnp.bfloat16)


def squares(context):
    wide = context.astype(jnp.float32)
    return jnp.sum(wide * wide, axis=-1)


def attend_kernel(seen_ref, q_ref, k_ref, v_ref, o_ref, bias_ref):
    tm = q_ref.shape[0]
    tp = k_ref.shape[1]
    scale = 1.0 / HD**0.5

    @pl.when(pl.program_id(1) == 0)
    def _():
        limit = seen_ref[...] * IMG_TOK
        allowed = lax.broadcasted_iota(jnp.int32, (tm, tp), 1).astype(jnp.float32) < limit
        bias_ref[...] = jnp.where(allowed, jnp.float32(0), jnp.float32(-1e30))

    bias = bias_ref[...]
    keys = k_ref[...]
    vals = v_ref[...]
    for pair in range(0, GROUP, 4):
        scores = []
        for g in range(pair, pair + 4):
            q = q_ref[:, g * HD : (g + 1) * HD]
            scores.append(jnp.dot(q, keys, preferred_element_type=jnp.float32) * scale + bias)
        for g, s in zip(range(pair, pair + 4), scores):
            top = jnp.max(s, axis=1, keepdims=True)
            w = jnp.exp(s - top)
            both = jnp.dot(w.astype(jnp.bfloat16), vals, preferred_element_type=jnp.float32)
            ctx = both[:, :HD] / both[:, HD : HD + 1]
            o_ref[:, g * HD : (g + 1) * HD] = ctx.astype(o_ref.dtype)


def attend(q, seen, keys, values):
    rows, width = q.shape
    tokens = keys.shape[0]
    padded = -(-tokens // 128) * 128
    kv_local = keys.shape[1] // HD
    kp = jnp.pad(keys, ((0, padded - tokens), (0, 0)))
    kp = kp.reshape(padded, kv_local, HD).transpose(1, 2, 0)
    vp = jnp.pad(values, ((0, padded - tokens), (0, 0)))
    vp = vp.reshape(padded, kv_local, HD).transpose(1, 0, 2)
    ones = jnp.zeros((kv_local, padded, HD), vp.dtype).at[:, :, 0].set(1)
    vp = jnp.concatenate([vp, ones], axis=2)
    tm = math.gcd(rows, 192)
    return pl.pallas_call(
        attend_kernel,
        grid=(rows // tm, kv_local),
        in_specs=[
            pl.BlockSpec((tm, 1), lambda i, k: (i, 0)),
            pl.BlockSpec((tm, GROUP * HD), lambda i, k: (i, k)),
            pl.BlockSpec((None, HD, padded), lambda i, k: (k, 0, 0)),
            pl.BlockSpec((None, padded, 2 * HD), lambda i, k: (k, 0, 0)),
        ],
        out_specs=pl.BlockSpec((tm, GROUP * HD), lambda i, k: (i, k)),
        scratch_shapes=[pltpu.VMEM((tm, padded), jnp.float32)],
        out_shape=jax.ShapeDtypeStruct((rows, width), jnp.bfloat16),
        cost_estimate=pl.CostEstimate(
            flops=4 * rows * width * padded,
            transcendentals=rows * (width // HD) * padded,
            bytes_accessed=4 * rows * width + 4 * padded * kv_local * HD,
        ),
    )(seen, q, kp, vp)


def power_kernel(x_ref, o_ref, slots, send_sem, recv_sem):
    doc = lax.axis_index("docs")
    col = lax.axis_index("mp")
    n = slots.shape[0]
    mesh_id = pl.DeviceIdType.MESH
    barrier = pltpu.get_barrier_semaphore()
    for d in range(1, n):
        pl.semaphore_signal(barrier, inc=1, device_id=(doc, lax.rem(col + d, n)), device_id_type=mesh_id)
    pl.semaphore_wait(barrier, n - 1)
    slots[col] = x_ref[...]
    copies = []
    for d in range(1, n):
        copy = pltpu.make_async_remote_copy(
            src_ref=x_ref,
            dst_ref=slots.at[col],
            send_sem=send_sem.at[d - 1],
            recv_sem=recv_sem.at[d - 1],
            device_id=(doc, lax.rem(col + d, n)),
            device_id_type=mesh_id,
        )
        copy.start()
        copies.append(copy)
    for d in range(1, n):
        copies[d - 1].wait_send()
        pltpu.make_async_copy(
            x_ref, slots.at[lax.rem(col + n - d, n)], recv_sem.at[d - 1]
        ).wait()
    total = slots[0]
    for i in range(1, n):
        total = total + slots[i]
    o_ref[...] = total


def power_sum(part):
    n = lax.axis_size("mp")
    row = part.reshape(1, -1)
    return pl.pallas_call(
        power_kernel,
        in_specs=[pl.BlockSpec(memory_space=pltpu.VMEM)],
        out_specs=pl.BlockSpec(memory_space=pltpu.VMEM),
        out_shape=jax.ShapeDtypeStruct(row.shape, row.dtype),
        scratch_shapes=[
            pltpu.VMEM((n,) + row.shape, row.dtype),
            pltpu.SemaphoreType.DMA((n - 1,)),
            pltpu.SemaphoreType.DMA((n - 1,)),
        ],
        compiler_params=pltpu.CompilerParams(collective_id=0, has_side_effects=True),
    )(row).reshape(part.shape)


def shards(queries, keys, values, owner_of_row, visible, gain):
    docs = lax.axis_size("docs")
    rows = queries.shape[0]
    width = queries.shape[1]
    cap = max(2, 3 * rows // (2 * docs))
    route = owner_of_row[:, 0]
    onehot = (route[:, None] == jnp.arange(docs, dtype=jnp.int32)[None, :]).astype(jnp.int32)
    before = jnp.cumsum(onehot, axis=0) - onehot
    rank = jnp.sum(before * onehot, axis=1)
    target = route * cap + rank
    place = (jnp.arange(docs * cap, dtype=jnp.int32)[:, None] == target[None, :]).astype(
        jnp.bfloat16
    )
    packed = jnp.dot(place, queries, preferred_element_type=jnp.float32).astype(jnp.bfloat16)
    seen = jnp.dot(place, visible.astype(jnp.bfloat16), preferred_element_type=jnp.float32)
    lanes = cap * width // 8
    slabs = packed.reshape(docs, 8, lanes)
    seen_tile = jnp.pad(seen.astype(jnp.bfloat16).reshape(docs, 1, cap), ((0, 0), (0, 7), (0, 128 - cap)))
    sent = jnp.concatenate([slabs, seen_tile], axis=2)
    arrived = lax.all_to_all(sent, "docs", split_axis=0, concat_axis=0, tiled=True)
    arrived_q = arrived[:, :, :lanes].reshape(docs * cap, width)
    arrived_seen = arrived[:, 0, lanes : lanes + cap].astype(jnp.float32).reshape(docs * cap, 1)
    context = attend(arrived_q, arrived_seen, keys, values)
    returned = lax.all_to_all(context.reshape(docs, 8, lanes), "docs", split_axis=0, concat_axis=0, tiled=True)
    flat_back = returned.reshape(docs * cap, width)
    mine = jnp.einsum("sr,sc->rc", place, flat_back, preferred_element_type=jnp.float32).astype(
        jnp.bfloat16
    )
    power = power_sum(squares(mine))
    return rescale(mine, power, gain)


def solution(mesh):
    return jax.shard_map(
        shards,
        mesh=mesh,
        in_specs=(
            P("docs", "mp"),
            P("docs", "mp"),
            P("docs", "mp"),
            P("docs", None),
            P("docs"),
            P("mp"),
        ),
        out_specs=P("docs", "mp"),
        check_vma=False,
    )
```
